256 devices in a mesh: pair: 32 (over x, z_hi, y), rows: 8 (over z_lo, core).
Axes of the slice: x: 4, y: 4, z: 8 (z_hi: 2, z_lo: 4; z = z_hi * 4 + z_lo), core: 2. Of those that a mesh axis runs over, the one named last changes fastest.
Arguments:
- samples: float32 [32768, 4096], P(('pair', 'rows')), may hold values from -400 to 400
- keep_mask: int32 [256, 8], P(('pair', 'rows')), may hold values 0 or 1
- keep_rate: float32 [8], replicated, may hold values from 0.5 to 1
Outputs:
- cosine: float32 [64, 512, 512], P('pair', 'rows')
The draws below stay inside these ranges and needn't reach their ends.
All inputs are finite; a program needn't handle non-finite values. No bound on the sum of `keep_mask` on one device may be relied on, other than what follows from the above.
Results may differ from the reference program's by a relative error of at most 0.00005.
Values sent between devices are 32-bit elements; how exact they have to be, the bound alone decides.
A program may use at most 128 MiB of HBM per device.

```python
import math
import jax
import jax.numpy as jnp
from jax import lax

BLOCKS = 8
BLOCK_COLS = 512
BLOCK_ROWS = 128
COLS = 4096
ROWS_ALL = 32768
ROW_BLOCKS = 256
TILES = 64


def draw_samples(key, part):
    key_noise = jax.random.fold_in(key, 11)
    key_scale = jax.random.fold_in(key, 12)
    noise = jnp.clip(jax.random.normal(key_noise, (ROWS_ALL, COLS + 1), jnp.float32), -6.0, 6.0)
    mixed = noise[:, :COLS] + 0.6 * noise[:, 1:]
    position = jnp.arange(ROWS_ALL, dtype=jnp.float32) / ROWS_ALL
    rising = jnp.exp(jnp.log(3.0) * position)
    factor = jnp.exp(jax.random.uniform(key_scale, (ROWS_ALL,), jnp.float32, jnp.log(0.5), jnp.log(2.0)))
    return (mixed * (factor * rising)[:, None]).astype(jnp.float32)


def with_ends(array, own_key, least, high):
    spot = [jax.random.randint(jax.random.fold_in(own_key, axis), (), 0, length) for axis, length in enumerate(array.shape)]
    longest = array.shape.index(max(array.shape))
    next_to = spot[:longest] + [(spot[longest] + 1) % array.shape[longest]] + spot[longest + 1:]
    return array.at[tuple(spot)].set(least).at[tuple(next_to)].set(high)


def setup_inputs(seed: int = 0) -> dict:
    streams_of = jax.random.split(jax.random.key(seed), 4)
    samples = draw_samples(jax.random.fold_in(streams_of[3], 71), 0)
    keep_mask = with_ends((jax.random.randint(streams_of[1], (ROW_BLOCKS, BLOCKS), 0, 4) < 3).astype(jnp.int32), jax.random.fold_in(streams_of[1], 1), 0, 1)
    keep_rate = jnp.clip(jnp.exp(jax.random.uniform(streams_of[2], (BLOCKS,), jnp.float32, math.log(0.5), math.log(1.0))), 0.5, 1.0)
    return dict(samples=samples, keep_mask=keep_mask, keep_rate=keep_rate)


EPS = 1e-06

def reference(samples, keep_mask, keep_rate):
    weights = keep_mask.astype(jnp.float32)
    masked = samples.reshape(ROW_BLOCKS, BLOCK_ROWS, BLOCKS, BLOCK_COLS) * weights[:, None, :, None]
    masked = masked.reshape(ROWS_ALL, COLS)
    col_norms = jnp.sqrt(lax.optimization_barrier(jnp.sum(samples * samples, axis=0)) + EPS)
    gram = jnp.dot(masked.T, masked, precision=lax.Precision.HIGHEST, preferred_element_type=jnp.float32)
    scale = jnp.repeat(keep_rate, BLOCK_COLS) * col_norms
    cosine = gram / (scale[:, None] * scale[None, :])
    cosine = cosine.reshape(BLOCKS, BLOCK_COLS, BLOCKS, BLOCK_COLS).transpose(0, 2, 1, 3)
    return cosine.reshape(TILES, BLOCK_COLS, BLOCK_COLS)
```

```python
import jax
import jax.numpy as jnp
from jax import lax
from jax.experimental import pallas as pl
from jax.experimental.pallas import tpu as pltpu
from jax.sharding import Mesh
from jax.sharding import PartitionSpec as P

AXES = ("x", "zh", "y", "zl", "c")
EPS = 1e-06
MESH = pl.DeviceIdType.MESH
OFFS = (2, 1, 3, 0)
ROWS = 136
F32 = jnp.float32
BF16 = jnp.bfloat16


def kernel(
    a_ref, w_ref, rate_ref, out_ref,
    R, LO, W, LTh, LTl, RH, RL, D, RSQ, YR, YRz, ZRy, ZRz, CF,
    ag_r, ag_s, rel_r, rel_s, two_s, sib_s, lo_r, lo_s, m_r, m_s,
    yr_r, yr_s, yz_r, yz_s, zy_r, zy_s, zz_r, zz_s, f_r, f_s,
):
    x, zh, y, zl, c = (lax.axis_index(a) for a in AXES)
    z = zh * 4 + zl
    oc = 1 - c

    def dev(dx=0, dy=0, dz=0, core=None):
        zz = (z + dz + 8) % 8
        return ((x + dx) % 4, zz // 4, (y + dy) % 4, zz % 4, c if core is None else core)

    pending = []

    def remote(src, dst, ss, rs, to):
        return pltpu.make_async_remote_copy(
            src_ref=src, dst_ref=dst, send_sem=ss, recv_sem=rs, device_id=to, device_id_type=MESH
        )

    def send(src, dst, ss, rs, to):
        copy = remote(src, dst, ss, rs, to)
        copy.start()
        pending.append(copy)

    def arrived(dst, rs, ss):
        remote(dst, dst, ss, rs, dev(core=oc)).wait_recv()

    partners = [dev(dx=d, core=k) for d in (1, 2, 3) for k in (0, 1)] + [dev(core=oc)]
    partners += [dev(dy=1), dev(dy=3), dev(dz=1), dev(dz=7)]
    bar = pltpu.get_barrier_semaphore()
    for p in partners:
        pl.semaphore_signal(bar, inc=1, device_id=p, device_id_type=MESH)
    pl.semaphore_wait(bar, len(partners))

    def cols(q, parity, r):
        start = pl.multiple_of((2 * q + parity) * 512 + r * 256, 256)
        return a_ref.at[:, pl.ds(start, 256)]

    def slot(dx, cs):
        return pl.ds(pl.multiple_of((dx * 2 + cs) * 128, 128), 128)

    def own_send(r, kq):
        for d in (1, 3):
            for k in (0, 1):
                q = (x + d + kq) % 4
                send(cols(q, k, r), R.at[kq, r, slot(4 - d, c), :],
                     ag_s.at[r, d // 2, k, kq], ag_r.at[r, 4 - d, c, kq], dev(dx=d, core=k))

    def sibling_send(r, kq):
        send(cols((x + kq) % 4, oc, r), R.at[kq, r, slot(0, c), :],
             sib_s.at[r, kq], ag_r.at[r, 0, c, kq], dev(core=oc))

    def wait_from(r, dx, cs, kq):
        arrived(R.at[kq, r, slot(dx, cs), :], ag_r.at[r, dx, cs, kq], ag_s.at[0, 0, 0, 0])

    for d in (1, 2, 3):
        for k in (0, 1):
            send(w_ref, W.at[(4 - d) * 2 + c], m_s.at[d * 2 + k], m_r.at[4 - d, c], dev(dx=d, core=k))
    send(w_ref, W.at[c], m_s.at[0], m_r.at[0, c], dev(core=oc))
    for r in (0, 1):
        sibling_send(r, 0)
        own_send(r, 0)
        for k in (0, 1):
            send(cols((x + 2) % 4, k, r), R.at[0, r, slot(2, c), :],
                 two_s.at[r, k], ag_r.at[r, 2, c, 0], dev(dx=2, core=k))
    for kq in (1, 2, 3):
        sibling_send(0, kq)
        own_send(0, kq)
    own_send(1, 1)

    W[c] = w_ref[...]
    for r in (0, 1):
        for kq in range(4):
            start = pl.multiple_of((2 * ((x + kq) % 4) + c) * 512 + r * 256, 256)
            R[kq, r, slot(0, c), :] = a_ref[:, pl.ds(start, 256)]

    def relay(r):
        for kq in (1, 2, 3):
            for cs in (0, 1):
                send(R.at[(kq + 1) % 4, r, slot(3, cs), 0:128], R.at[kq, r, slot(2, cs), 0:128],
                     rel_s.at[r, 0, cs, kq], rel_r.at[r, 0, cs, kq], dev(dx=1))
                send(R.at[kq - 1, r, slot(1, cs), 128:256], R.at[kq, r, slot(2, cs), 128:256],
                     rel_s.at[r, 1, cs, kq], rel_r.at[r, 1, cs, kq], dev(dx=3))

    def wait_neighbours(r):
        for kq in (1, 2, 3):
            for cs in (0, 1):
                wait_from(r, 1, cs, kq)
                wait_from(r, 3, cs, kq)

    def wait_rest(r):
        for kq in (1, 2, 3):
            wait_from(r, 0, oc, kq)
            for cs in (0, 1):
                for h in (0, 1):
                    arrived(R.at[kq, r, slot(2, cs), h * 128 : h * 128 + 128],
                            rel_r.at[r, h, cs, kq], rel_s.at[0, 0, 0, 1])

    for r in (0, 1):
        wait_from(r, 0, oc, 0)
        for dx in (1, 2, 3):
            for cs in (0, 1):
                wait_from(r, dx, cs, 0)
        send(R.at[0, r], LO.at[r], lo_s.at[r], lo_r.at[r], dev(core=oc))
    arrived(W.at[oc], m_r.at[0, oc], m_s.at[0])
    for dx in (1, 2, 3):
        for cs in (0, 1):
            arrived(W.at[dx * 2 + cs], m_r.at[dx, cs], m_s.at[0])

    def left(src, r, parity):
        block = 2 * x + parity
        base = parity * 512 + r * 256

        def step(k, squares):
            rows = pl.ds(pl.multiple_of(k * 128, 128), 128)
            raw = src[rows, :]
            weight = W[k, pl.ds(block, 1), :]
            for h in (0, 1):
                part = raw[:, h * 128 : h * 128 + 128] * weight
                turned = part.T
                high = turned.astype(BF16)
                low = (turned - high.astype(F32)).astype(BF16)
                at = pl.ds(pl.multiple_of(base + h * 128, 128), 128)
                LTh[at, rows] = high
                LTl[at, rows] = low
            return squares + jnp.sum(raw * raw, axis=0, keepdims=True)

        squares = lax.fori_loop(0, 8, step, jnp.zeros((1, 256), F32))
        for h in (0, 1):
            RSQ[parity * 4 + r * 2 + h] = squares[:, h * 128 : h * 128 + 128]

    for r in (0, 1):
        left(R.at[0, r], r, c)
    for r in (0, 1):
        arrived(LO.at[r], lo_r.at[r], lo_s.at[0])
        left(LO.at[r], r, oc)

    lane_row = lax.broadcasted_iota(jnp.int32, (8, 128), 0)

    def product(r, k, kq):
        src = R.at[kq, r]
        block = 2 * ((x + kq) % 4) + c

        def split(i, squares):
            rows = pl.ds(pl.multiple_of(i * 128, 128), 128)
            raw = src[rows, :]
            weight = W[i, pl.ds(block, 1), :]
            part = raw * jnp.concatenate([weight, weight], axis=1)
            high = part.astype(BF16)
            RH[rows, :] = high
            RL[rows, :] = (part - high.astype(F32)).astype(BF16)
            return squares + jnp.sum(raw * raw, axis=0, keepdims=True)

        squares = lax.fori_loop(0, 8, split, jnp.zeros((1, 256), F32))

        def rows_of(m, carry):
            at = pl.ds(pl.multiple_of(m * 256, 256), 256)
            lh = LTh[at, :]
            ll = LTl[at, :]
            rh = RH[...]
            acc = jnp.dot(lh, rh, preferred_element_type=F32)
            acc += jnp.dot(ll, rh, preferred_element_type=F32)
            acc += jnp.dot(lh, RL[...], preferred_element_type=F32)
            for i in (0, 1):
                for s in (0, 1):
                    D[r, s, k, 2 * m + i, 0:128, :] = acc[i * 128 : i * 128 + 128, s * 128 : s * 128 + 128]
                    extra = jnp.where(lane_row == 0, squares[:, s * 128 : s * 128 + 128], 0.0)
                    D[r, s, k, 2 * m + i, 128:ROWS, :] = jnp.where(lane_row == 1, RSQ[2 * m + i], extra)
            return carry

        lax.fori_loop(0, 4, rows_of, 0)

    def z_chain(chunk, buf, rs, ss, turn):
        def go(zd, j, way):
            send(chunk((z + zd * turn + 8) % 8), buf.at[j], ss.at[j], rs.at[j], dev(dz=way * turn))

        def take(j, zd):
            arrived(buf.at[j], rs.at[j], ss.at[0])
            ref = chunk((z + zd * turn + 8) % 8)
            ref[...] += buf[j]

        def start():
            go(4, 0, 1)
            go(-3, 4, -1)

        def step1():
            take(0, 3)
            go(3, 1, 1)
            take(4, -2)
            go(-2, 5, -1)

        def step2():
            take(1, 2)
            go(2, 2, 1)
            take(5, -1)
            go(-1, 6, -1)

        def step3():
            take(2, 1)
            go(1, 3, 1)
            take(6, 0)

        def finish():
            take(3, 0)

        return start, step1, step2, step3, finish

    def zz(r, k):
        return z_chain(lambda zd: D.at[r, 1, k, zd], ZRz.at[r, k], zz_r.at[r, k], zz_s.at[r, k],
                       1 - 2 * (k % 2))

    def zy(r):
        return z_chain(lambda zd: D.at[r, 0, 3, zd], ZRy.at[r], zy_r.at[r], zy_s.at[r], 1 - 2 * r)

    def y_chain(chunk, buf, rs, ss, turn):
        near, far = (1, 2) if turn == 1 else (2, 1)

        def go(k, j, way):
            send(chunk(k), buf.at[j], ss.at[j], rs.at[j], dev(dy=(way * turn) % 4))

        def take(j, k):
            arrived(buf.at[j], rs.at[j], ss.at[0])
            ref = chunk(k)
            ref[...] += buf[j]

        def start():
            go(0, 0, 1)

        def direct():
            go(far, 2, -1)

        def forward():
            take(0, near)
            go(near, 1, 1)

        def finish():
            take(2, 3)
            take(1, 3)

        return start, direct, forward, finish

    def yy(r, t):
        return y_chain(lambda k: D.at[r, 0, k, t * 4 : t * 4 + 4], YR.at[r, t], yr_r.at[r, t],
                       yr_s.at[r, t], 1 - 2 * t)

    def yz(r):
        return y_chain(lambda k: D.at[r, 1, k, z], YRz.at[r], yz_r.at[r], yz_s.at[r], 1 - 2 * r)

    mine = (x - y + 4) % 4
    k_mine = jnp.where(mine == 2, 0, jnp.where(mine == 1, 1, jnp.where(mine == 3, 2, 3)))

    def rest(r, k):
        kq = (y + OFFS[k] - x + 4) % 4

        @pl.when(kq != 0)
        def _():
            product(r, k, kq)

    yy_chains = {(r, t): yy(r, t) for r in (0, 1) for t in (0, 1)}
    yz_chains = {r: yz(r) for r in (0, 1)}
    zz_chains = {(r, k): zz(r, k) for r in (0, 1) for k in range(4)}
    zy_chains = {r: zy(r) for r in (0, 1)}

    for r in (0, 1):
        product(r, k_mine, 0)

    wait_neighbours(0)
    relay(0)
    for kq in (2, 3):
        own_send(1, kq)
    for kq in (1, 2, 3):
        sibling_send(1, kq)
    wait_rest(0)

    def compute(r):
        rest(r, 0)
        zz_chains[r, 0][0]()
        for t in (0, 1):
            yy_chains[r, t][0]()
        rest(r, 1)
        zz_chains[r, 1][0]()
        yy_chains[r, 1][1]()
        rest(r, 2)
        zz_chains[r, 2][0]()
        yy_chains[r, 0][1]()
        rest(r, 3)
        zz_chains[r, 3][0]()

    def z_round(r, j):
        for k in range(4):
            zz_chains[r, k][j]()

    def middle(r):
        z_round(r, 1)
        for t in (0, 1):
            yy_chains[r, t][2]()
        z_round(r, 2)

    def end(r):
        z_round(r, 3)
        for t in (0, 1):
            yy_chains[r, t][3]()
        zy_chains[r][0]()
        z_round(r, 4)
        yz_chains[r][0]()
        yz_chains[r][1]()
        zy_chains[r][1]()
        yz_chains[r][2]()
        zy_chains[r][2]()
        zy_chains[r][3]()
        yz_chains[r][3]()
        zy_chains[r][4]()

    compute(0)
    middle(0)
    wait_neighbours(1)
    relay(1)
    end(0)
    wait_rest(1)
    compute(1)
    middle(1)
    end(1)

    row_rate = rate_ref[2 * x + z // 4]
    col_rate = rate_ref[2 * y + c]
    row_scale = row_rate * jnp.sqrt(D[0, 0, 3, z, 129:130, :] + EPS)
    row_scale = jnp.broadcast_to(row_scale, (128, 128)).T
    for r in (0, 1):
        for s in (0, 1):
            col_scale = col_rate * jnp.sqrt(D[r, s, 3, z, 128:129, :] + EPS)
            at = r * 256 + s * 128
            CF[:, at : at + 128] = D[r, s, 3, z, 0:128, :] / (row_scale * col_scale)
    half = pl.ds(pl.multiple_of(oc * 64, 64), 64)
    send(CF.at[half, :], out_ref.at[c], f_s, f_r, dev(core=oc))
    out_ref[c] = CF[pl.ds(pl.multiple_of(c * 64, 64), 64), :]
    arrived(out_ref.at[oc], f_r, f_s)
    for copy in pending:
        copy.wait_send()


def per_device(samples, keep_mask, keep_rate):
    weights = jnp.broadcast_to(keep_mask.astype(F32).reshape(8, 1), (8, 128))
    dma = pltpu.SemaphoreType.DMA
    vmem = pltpu.VMEM
    return pl.pallas_call(
        kernel,
        out_shape=jax.ShapeDtypeStruct((2, 64, 512), F32),
        in_specs=[
            pl.BlockSpec(memory_space=pltpu.VMEM),
            pl.BlockSpec(memory_space=pltpu.VMEM),
            pl.BlockSpec(memory_space=pltpu.SMEM),
        ],
        out_specs=pl.BlockSpec(memory_space=pltpu.VMEM),
        scratch_shapes=[
            vmem((4, 2, 1024, 256), F32),
            vmem((2, 1024, 256), F32),
            vmem((8, 8, 128), F32),
            vmem((1024, 1024), BF16),
            vmem((1024, 1024), BF16),
            vmem((1024, 256), BF16),
            vmem((1024, 256), BF16),
            vmem((2, 2, 4, 8, ROWS, 128), F32),
            vmem((8, 1, 128), F32),
            vmem((2, 2, 3, 4, ROWS, 128), F32),
            vmem((2, 3, ROWS, 128), F32),
            vmem((2, 7, ROWS, 128), F32),
            vmem((2, 4, 7, ROWS, 128), F32),
            vmem((128, 512), F32),
            dma((2, 4, 2, 4)),
            dma((2, 2, 2, 4)),
            dma((2, 2, 2, 4)),
            dma((2, 2, 2, 4)),
            dma((2, 2)),
            dma((2, 4)),
            dma((2,)),
            dma((2,)),
            dma((4, 2)),
            dma((8,)),
            dma((2, 2, 3)),
            dma((2, 2, 3)),
            dma((2, 3)),
            dma((2, 3)),
            dma((2, 7)),
            dma((2, 7)),
            dma((2, 4, 7)),
            dma((2, 4, 7)),
            dma,
            dma,
        ],
        compiler_params=pltpu.CompilerParams(
            collective_id=0, has_side_effects=True, vmem_limit_bytes=60 << 20
        ),
        name="sampled_gram",
    )(samples, weights, keep_rate)


def solution(mesh):
    finer = Mesh(mesh.devices.reshape(4, 2, 4, 4, 2), AXES)
    rows = P(AXES, None)
    return jax.shard_map(
        per_device,
        mesh=finer,
        in_specs=(rows, rows, P()),
        out_specs=P(("x", "zh", "y"), ("zl", "c"), None),
        check_vma=False,
    )
```

```python
import jax
import jax.numpy as jnp
from jax import lax
from jax.experimental import pallas as pl
from jax.experimental.pallas import tpu as pltpu
from jax.sharding import Mesh
from jax.sharding import PartitionSpec as P

AXES = ("x", "zh", "y", "zl", "c")
EPS = 1e-06
MESH = pl.DeviceIdType.MESH
OFFS = (2, 1, 3, 0)
PLACE = {0: 0, 1: 1, 3: 2, 2: 3}
GROUPS = (((1, 1), (1, 2), (1, 3)), ((0, 1), (0, 2), (0, 3)), ((2, 1), (2, 2), (2, 3)), ((3, 1), (3, 2), (3, 3)))
AHEAD = 2
SCHEDULE = (
    ("mul", (0, 0), (3, 0)), ("z", 3, 0, 0), ("z", 0, 0, 0), ("mul", (1, 0), (2, 0)), ("pass", 0),
    ("z", 3, 0, 1), ("z", 0, 0, 1), ("z", 3, 0, 2), ("mul", (1, 1), (1, 2)), ("z", 0, 0, 2), ("mul", (1, 3)),
    ("pass", 1), ("y", 1, 1, 1), ("y", 1, 1, 0), ("y", 1, 0, 1), ("y", 1, 0, 0), ("z", 3, 0, 3),
    ("z", 0, 0, 3), ("z", 3, 0, 4), ("z", 0, 0, 4), ("mul", (0, 1), (0, 2)), ("y", 1, 1, 2), ("z", 0, 2, 0),
    ("z", 0, 1, 0), ("mul", (0, 3)), ("pass", 2), ("z", 0, 3, 0), ("z", 0, 2, 1), ("y", 1, 0, 2),
    ("z", 0, 1, 1), ("z", 0, 3, 1), ("z", 0, 2, 2), ("mul", (2, 1), (2, 2)), ("y", 1, 1, 3), ("pass", 3),
    ("z", 0, 1, 2), ("mul", (2, 3)), ("y", 2, 0, 0), ("y", 2, 1, 0), ("y", 1, 0, 3), ("zy", 1, 0),
    ("y", 2, 1, 1), ("y", 2, 0, 1), ("z", 0, 3, 2), ("z", 0, 2, 3), ("z", 0, 1, 3), ("mul", (3, 1), (3, 2)),
    ("zy", 1, 1), ("z", 3, 1, 0), ("z", 3, 2, 0), ("mul", (3, 3)), ("z", 3, 3, 0), ("z", 0, 3, 3),
    ("z", 0, 2, 4), ("z", 0, 1, 4), ("y", 2, 0, 2), ("y", 2, 1, 2), ("zy", 1, 2), ("z", 3, 1, 1),
    ("z", 3, 2, 1), ("z", 3, 3, 1), ("z", 0, 3, 4), ("yz", 0, 0), ("yz", 0, 1), ("zy", 1, 3), ("z", 3, 1, 2),
    ("y", 2, 1, 3), ("y", 2, 0, 3), ("zy", 2, 0), ("z", 3, 2, 2), ("yz", 0, 2), ("z", 3, 3, 2), ("zy", 1, 4),
    ("z", 3, 1, 3), ("zy", 2, 1), ("yz", 0, 3), ("z", 3, 2, 3), ("z", 3, 3, 3), ("z", 3, 1, 4),
    ("z", 3, 2, 4), ("zy", 2, 2), ("z", 3, 3, 4), ("yz", 3, 0), ("yz", 3, 1), ("zy", 2, 3), ("yz", 3, 2),
    ("zy", 2, 4), ("yz", 3, 3),
)
ROWS = 136
F32 = jnp.float32
BF16 = jnp.bfloat16


def kernel(
    a_ref, mask_ref, rate_ref, out_ref,
    R, LO, W, LTh, LTl, RH, RL, D, RSQ, YR, YRz, ZRy, ZRz, CF,
    ag_r, rel_r, lo_r, m_r, yr_r, yz_r, zy_r, zz_r, f_r,
    own_s, rel_s, sib_s, lo_s, m_s, yr_s, yz_s, zy_s, zz_s, f_s,
):
    x, zh, y, zl, c = (lax.axis_index(a) for a in AXES)
    z = zh * 4 + zl
    oc = 1 - c

    def dev(dx=0, dy=0, dz=0, core=None):
        zz = (z + dz + 8) % 8
        return ((x + dx) % 4, zz // 4, (y + dy) % 4, zz % 4, c if core is None else core)

    def remote(src, dst, ss, rs, to):
        return pltpu.make_async_remote_copy(
            src_ref=src, dst_ref=dst, send_sem=ss, recv_sem=rs, device_id=to, device_id_type=MESH
        )

    def send(src, dst, ss, rs, to):
        remote(src, dst, ss, rs, to).start()

    def arrived(dst, rs):
        remote(dst, dst, f_s, rs, dev(core=oc)).wait_recv()

    def all_sent(ref, ss):
        remote(ref, ref, ss, f_r, dev(core=oc)).wait_send()

    def slot(dx, cs):
        return PLACE[dx] * 2 + cs

    lane_row = lax.broadcasted_iota(jnp.int32, (8, 128), 0)
    weights = jnp.zeros((8, 128), F32)
    for b in range(8):
        weights = jnp.where(lane_row == b, mask_ref[0, b].astype(F32), weights)
    W[slot(0, c)] = weights
    w_ref = W.at[slot(0, c)]

    partners = [dev(dx=d, core=k) for d in (1, 2, 3) for k in (0, 1)] + [dev(core=oc)]
    partners += [dev(dy=1), dev(dy=3), dev(dz=1), dev(dz=7)]
    bar = pltpu.get_barrier_semaphore()
    for p in partners:
        pl.semaphore_signal(bar, inc=1, device_id=p, device_id_type=MESH)
    pl.semaphore_wait(bar, len(partners))

    def cols(q, parity, r):
        return pl.ds(pl.multiple_of((2 * q + parity) * 512 + r * 128, 128), 128)

    def rows_at(dx, cs, half=None):
        first = slot(dx, cs) * 128 + (64 if half == 1 else 0)
        return pl.ds(pl.multiple_of(first, 64), 128 if half is None else 64)

    def half_rows(half):
        return pl.ds(64 if half == 1 else 0, 128 if half is None else 64)

    def own_part(r, kq, d, half):
        for k in (0, 1):
            q = (x + d + kq) % 4
            send(a_ref.at[half_rows(half), cols(q, k, r)], R.at[kq, r, rows_at(4 - d, c, half), :],
                 own_s.at[d // 2], ag_r.at[r, 4 - d, c, kq, half or 0], dev(dx=d, core=k))

    def own_send(r, kq):
        own_part(r, kq, 1, 1 if kq == 1 else None)
        own_part(r, kq, 3, 0 if kq == 3 else None)
        sibling_send(r, kq)

    def sibling_send(r, kq):
        send(a_ref.at[:, cols((x + kq) % 4, oc, r)], R.at[kq, r, rows_at(0, c), :],
             sib_s, ag_r.at[r, 0, c, kq, 0], dev(core=oc))

    def wait_part(r, dx, cs, kq, half):
        arrived(R.at[kq, r, rows_at(dx, cs, half), :], ag_r.at[r, dx, cs, kq, half or 0])

    def relay(r, kq):
        for cs in (0, 1):
            send(R.at[(kq + 1) % 4, r, rows_at(3, cs, 0), :], R.at[kq, r, rows_at(2, cs, 0), :],
                 rel_s.at[0], rel_r.at[r, 0, cs, kq], dev(dx=1))
            send(R.at[(kq + 3) % 4, r, rows_at(1, cs, 1), :], R.at[kq, r, rows_at(2, cs, 1), :],
                 rel_s.at[1], rel_r.at[r, 1, cs, kq], dev(dx=3))

    def wait_relayed(r, kq):
        for cs in (0, 1):
            for h in (0, 1):
                arrived(R.at[kq, r, rows_at(2, cs, h), :], rel_r.at[r, h, cs, kq])

    def wait_neighbours(r, kq):
        for cs in (0, 1):
            wait_part(r, 3, cs, kq, 1 if kq == 1 else None)
            wait_part(r, 1, cs, kq, 0 if kq == 3 else None)

    def wait_rest(r, kq):
        wait_part(r, 0, oc, kq, None)
        wait_relayed(r, kq)

    units = [u for group in GROUPS for u in group]
    sent = [0]

    def own_sends(upto):
        for u in units[sent[0] : upto]:
            own_send(*u)
        sent[0] = max(sent[0], upto)

    def pass_on(i):
        for u in GROUPS[i]:
            wait_neighbours(*u)
        for u in GROUPS[i]:
            relay(*u)
        own_sends(sum(len(group) for group in GROUPS[: i + 2]) + AHEAD)

    for d in (1, 2, 3):
        for k in (0, 1):
            send(w_ref, W.at[slot(4 - d, c)], m_s.at[d * 2 + k], m_r.at[4 - d, c], dev(dx=d, core=k))
    send(w_ref, W.at[slot(0, c)], m_s.at[0], m_r.at[0, c], dev(core=oc))
    for r in range(4):
        own_part(r, 1, 1, 0)
        own_part(r, 3, 3, 1)
    for r in range(4):
        own_part(r, 0, 1, None)
        own_part(r, 0, 3, None)
        sibling_send(r, 0)

    for r in range(4):
        for kq in range(4):
            R[kq, r, rows_at(0, c), :] = a_ref[:, cols((x + kq) % 4, c, r)]

    for r in range(4):
        for cs in (0, 1):
            wait_part(r, 3, cs, 1, 0)
            wait_part(r, 1, cs, 3, 1)
        relay(r, 0)
    own_sends(len(GROUPS[0]) + AHEAD)

    def left(src, r, parity, first, last):
        block = 2 * x + parity
        at = pl.ds(pl.multiple_of(parity * 512 + r * 128, 128), 128)

        def step(k, squares):
            rows = pl.ds(pl.multiple_of(k * 128, 128), 128)
            raw = src[rows, :]
            turned = (raw * W[k, pl.ds(block, 1), :]).T
            high = turned.astype(BF16)
            LTh[at, rows] = high
            LTl[at, rows] = (turned - high.astype(F32)).astype(BF16)
            return squares + jnp.sum(raw * raw, axis=0, keepdims=True)

        before = RSQ[parity * 4 + r] if first else jnp.zeros((1, 128), F32)
        RSQ[parity * 4 + r] = lax.fori_loop(first, last, step, before)

    for r in range(4):
        wait_part(r, 0, oc, 0, None)
        for cs in (0, 1):
            wait_part(r, 1, cs, 0, None)
            wait_part(r, 3, cs, 0, None)
        send(R.at[0, r, 0:768], LO.at[r, 0:768], lo_s, lo_r.at[r, 0], dev(core=oc))
    arrived(W.at[slot(0, oc)], m_r.at[0, oc])
    for dx in (1, 2, 3):
        for cs in (0, 1):
            arrived(W.at[slot(dx, cs)], m_r.at[dx, cs])
    for r in range(4):
        left(R.at[0, r], r, c, 0, 6)
        arrived(LO.at[r, 0:768], lo_r.at[r, 0])
        left(LO.at[r], r, oc, 0, 6)
    for r in range(4):
        wait_relayed(r, 0)
        send(R.at[0, r, 768:1024], LO.at[r, 768:1024], lo_s, lo_r.at[r, 1], dev(core=oc))
        left(R.at[0, r], r, c, 6, 8)
    for r in range(4):
        arrived(LO.at[r, 768:1024], lo_r.at[r, 1])
        left(LO.at[r], r, oc, 6, 8)

    def product(*units):
        width = 128 * len(units)
        squares = []
        for j, (r, kq) in enumerate(units):
            src = R.at[kq, r]
            block = 2 * ((x + kq) % 4) + c
            at = slice(j * 128, j * 128 + 128)

            def split(i, total):
                rows = pl.ds(pl.multiple_of(i * 128, 128), 128)
                raw = src[rows, :]
                part = raw * W[i, pl.ds(block, 1), :]
                high = part.astype(BF16)
                RH[rows, at] = high
                RL[rows, at] = (part - high.astype(F32)).astype(BF16)
                return total + jnp.sum(raw * raw, axis=0, keepdims=True)

            squares.append(lax.fori_loop(0, 8, split, jnp.zeros((1, 128), F32)))

        def rows_of(m, carry):
            at = pl.ds(pl.multiple_of(m * 512, 512), 512)
            lh = LTh[at, :]
            rh = RH[:, 0:width]
            acc = jnp.dot(lh, rh, preferred_element_type=F32)
            acc += jnp.dot(LTl[at, :], rh, preferred_element_type=F32)
            acc += jnp.dot(lh, RL[:, 0:width], preferred_element_type=F32)
            for i in range(4):
                zd = 4 * m + i
                for j, (r, kq) in enumerate(units):
                    D[r, kq, zd, 0:128, :] = acc[i * 128 : i * 128 + 128, j * 128 : j * 128 + 128]
                    extra = jnp.where(lane_row == 0, squares[j], 0.0)
                    D[r, kq, zd, 128:ROWS, :] = jnp.where(lane_row == 1, RSQ[zd], extra)
            return carry

        lax.fori_loop(0, 2, rows_of, 0)

    def z_chain(chunk, buf, rs, ss, turn):
        def go(zd, j, way):
            send(chunk((z + zd * turn + 8) % 8), buf.at[j], ss, rs.at[j], dev(dz=way * turn))

        def take(j, zd):
            arrived(buf.at[j], rs.at[j])
            ref = chunk((z + zd * turn + 8) % 8)
            ref[...] += buf[j]

        def start():
            go(4, 0, 1)
            go(-3, 4, -1)

        def step1():
            take(0, 3)
            go(3, 1, 1)
            take(4, -2)
            go(-2, 5, -1)

        def step2():
            take(1, 2)
            go(2, 2, 1)
            take(5, -1)
            go(-1, 6, -1)

        def step3():
            take(2, 1)
            go(1, 3, 1)
            take(6, 0)

        def finish():
            take(3, 0)

        return start, step1, step2, step3, finish

    def y_chain(chunk, buf, rs, ss, turn):
        near, far = (1, 2) if turn == 1 else (2, 1)

        def go(k, j, way):
            send(chunk(k), buf.at[j], ss, rs.at[j], dev(dy=(way * turn) % 4))

        def take(j, k):
            arrived(buf.at[j], rs.at[j])
            ref = chunk(k)
            ref[...] += buf[j]

        def start():
            go(0, 0, 1)

        def direct():
            go(far, 2, -1)

        def forward():
            take(0, near)
            go(near, 1, 1)

        def finish():
            take(2, 3)
            take(1, 3)

        return start, direct, forward, finish

    kqs = [(y + off - x + 4) % 4 for off in OFFS]

    def zz(r, kq):
        i = r // 3
        return z_chain(lambda zd: D.at[r, kq, zd], ZRz.at[i, kq], zz_r.at[i, kq], zz_s.at[i, kq],
                       1 - 2 * ((kq + i) % 2))

    def zy(r):
        i = r - 1
        return z_chain(lambda zd: D.at[r, kqs[3], zd], ZRy.at[i], zy_r.at[i], zy_s.at[i], 1 - 2 * i)

    def yy(r, t):
        i = r - 1
        return y_chain(lambda k: D.at[r, kqs[k], t * 4 : t * 4 + 4], YR.at[i, t], yr_r.at[i, t],
                       yr_s.at[i, t], 1 - 2 * t)

    def yz(r):
        i = r // 3
        return y_chain(lambda k: D.at[r, kqs[k], z], YRz.at[i], yz_r.at[i], yz_s.at[i], 1 - 2 * i)

    ZZ = {(r, kq): zz(r, kq) for r in (0, 3) for kq in range(4)}
    ZY = {r: zy(r) for r in (1, 2)}
    YY = {(r, t): yy(r, t) for r in (1, 2) for t in (0, 1)}
    YZ = {r: yz(r) for r in (0, 3)}

    def y_begin(r, early):
        for k in range(3):

            @pl.when((kqs[k] == 0) == early)
            def _():
                if k == 0:
                    YY[r, 0][0]()
                    YY[r, 1][0]()
                else:
                    YY[r, 2 - k][1]()

    begun = set()
    for name, *key in SCHEDULE:
        if name == "mul":
            for u in key:
                if u[1]:
                    wait_rest(*u)
            product(*key)
            for r, kq in key:
                if kq == 0 and r in (1, 2):
                    y_begin(r, True)
        elif name == "pass":
            pass_on(*key)
        elif name == "z":
            ZZ[key[0], key[1]][key[2]]()
        elif name == "zy":
            ZY[key[0]][key[1]]()
        elif name == "yz":
            YZ[key[0]][key[1]]()
        elif key[2] > 1:
            YY[key[0], key[1]][key[2]]()
        elif key[0] not in begun:
            begun.add(key[0])
            y_begin(key[0], False)

    own = kqs[3]
    row_rate = rate_ref[2 * x + z // 4]
    col_rate = rate_ref[2 * y + c]
    row_scale = row_rate * jnp.sqrt(D[0, own, z, 129:130, :] + EPS)
    row_scale = jnp.broadcast_to(row_scale, (128, 128)).T
    for r in range(4):
        col_scale = col_rate * jnp.sqrt(D[r, own, z, 128:129, :] + EPS)
        CF[:, r * 128 : r * 128 + 128] = D[r, own, z, 0:128, :] / (row_scale * col_scale)
    half = pl.ds(pl.multiple_of(oc * 64, 64), 64)
    send(CF.at[half, :], out_ref.at[c], f_s, f_r, dev(core=oc))
    out_ref[c] = CF[pl.ds(pl.multiple_of(c * 64, 64), 64), :]
    arrived(out_ref.at[oc], f_r)
    all_sent(CF.at[half, :], f_s)
    for i in range(2):
        all_sent(a_ref, own_s.at[i])
        all_sent(a_ref.at[:, 0:2048], rel_s.at[i])
        all_sent(YRz.at[i], yz_s.at[i])
        all_sent(ZRy.at[i], zy_s.at[i])
        for t in range(2):
            all_sent(YR.at[i, t], yr_s.at[i, t])
        for kq in range(4):
            all_sent(ZRz.at[i, kq], zz_s.at[i, kq])
    all_sent(a_ref.at[:, 0:2048], sib_s)
    all_sent(LO, lo_s)
    for i in [0] + list(range(2, 8)):
        all_sent(w_ref, m_s.at[i])


def per_device(samples, keep_mask, keep_rate):
    dma = pltpu.SemaphoreType.DMA
    vmem = pltpu.VMEM
    return pl.pallas_call(
        kernel,
        out_shape=jax.ShapeDtypeStruct((2, 64, 512), F32),
        in_specs=[
            pl.BlockSpec(memory_space=pltpu.VMEM),
            pl.BlockSpec(memory_space=pltpu.SMEM),
            pl.BlockSpec(memory_space=pltpu.SMEM),
        ],
        out_specs=pl.BlockSpec(memory_space=pltpu.VMEM),
        scratch_shapes=[
            vmem((4, 4, 1024, 128), F32),
            vmem((4, 1024, 128), F32),
            vmem((8, 8, 128), F32),
            vmem((1024, 1024), BF16),
            vmem((1024, 1024), BF16),
            vmem((1024, 256), BF16),
            vmem((1024, 256), BF16),
            vmem((4, 4, 8, ROWS, 128), F32),
            vmem((8, 1, 128), F32),
            vmem((2, 2, 3, 4, ROWS, 128), F32),
            vmem((2, 3, ROWS, 128), F32),
            vmem((2, 7, ROWS, 128), F32),
            vmem((2, 4, 7, ROWS, 128), F32),
            vmem((128, 512), F32),
            dma((4, 4, 2, 4, 2)),
            dma((4, 2, 2, 4)),
            dma((4, 2)),
            dma((4, 2)),
            dma((2, 2, 3)),
            dma((2, 3)),
            dma((2, 7)),
            dma((2, 4, 7)),
            dma,
            dma((2,)),
            dma((2,)),
            dma,
            dma,
            dma((8,)),
            dma((2, 2)),
            dma((2,)),
            dma((2,)),
            dma((2, 4)),
            dma,
        ],
        compiler_params=pltpu.CompilerParams(
            collective_id=0, has_side_effects=True, vmem_limit_bytes=60 << 20
        ),
        name="sampled_gram",
    )(samples, keep_mask, keep_rate)


def solution(mesh):
    finer = Mesh(mesh.devices.reshape(4, 2, 4, 4, 2), AXES)
    rows = P(AXES, None)
    return jax.shard_map(
        per_device,
        mesh=finer,
        in_specs=(rows, rows, P()),
        out_specs=P(("x", "zh", "y"), ("zl", "c"), None),
        check_vma=False,
    )
```

```python
import jax
import jax.numpy as jnp
from jax import lax
from jax.experimental import pallas as pl
from jax.experimental.pallas import tpu as pltpu
from jax.sharding import Mesh
from jax.sharding import PartitionSpec as P

AXES = ("x", "zh", "y", "zl", "c")
EPS = 1e-06
MESH = pl.DeviceIdType.MESH
OFFS = (2, 1, 3, 0)
PLACE = {0: 0, 1: 1, 3: 2, 2: 3}
GROUPS = (((1, 1), (2, 1)), ((0, 1), (3, 1)), ((1, 2), (2, 2)), ((0, 2), (3, 2)))
AHEAD = 1
SCHEDULE = (
    ("mul", (1, 0), (2, 0)), ("y", 2, 0, 0, 0), ("y", 1, 0, 1, 0), ("y", 1, 0, 0, 0), ("y", 2, 0, 1, 0),
    ("mul", (0, 0), (3, 0)), ("pass", 0), ("z", 3, 0, 0), ("z", 0, 0, 0), ("z", 3, 0, 1),
    ("mul", (1, 1), (2, 1)), ("y", 1, 1, 1, 0), ("y", 2, 1, 1, 0), ("y", 1, 1, 0, 0), ("y", 2, 1, 0, 0),
    ("y", 2, 0, 0, 1), ("z", 0, 0, 1), ("y", 1, 0, 1, 1), ("pass", 1), ("z", 3, 0, 2), ("y", 1, 0, 0, 1),
    ("z", 0, 0, 2), ("y", 2, 0, 1, 1), ("mul", (0, 1), (3, 1)), ("y", 1, 1, 1, 1), ("z", 3, 1, 0),
    ("z", 0, 1, 0), ("z", 3, 0, 3), ("pass", 2), ("z", 0, 0, 3), ("y", 2, 1, 1, 1), ("z", 3, 1, 1),
    ("y", 1, 1, 0, 1), ("y", 2, 1, 0, 1), ("z", 0, 1, 1), ("mul", (1, 2), (2, 2)), ("y", 1, 2, 1, 0),
    ("y", 1, 0, 1, 2), ("z", 3, 0, 4), ("yz", 3, 0, 0), ("y", 2, 2, 0, 0), ("y", 2, 0, 0, 2), ("pass", 3),
    ("y", 2, 2, 1, 0), ("z", 3, 1, 2), ("y", 1, 2, 0, 0), ("z", 0, 0, 4), ("yz", 0, 0, 0), ("y", 1, 0, 0, 2),
    ("y", 2, 0, 1, 2), ("zy", 1, 0, 0), ("zy", 2, 0, 0), ("z", 0, 1, 2), ("y", 1, 1, 1, 2), ("z", 3, 1, 3),
    ("y", 1, 1, 0, 2), ("zy", 1, 1, 0), ("y", 2, 1, 1, 2), ("yz", 3, 0, 1), ("mul", (0, 2), (3, 2)),
    ("zy", 1, 0, 1), ("zy", 2, 0, 1), ("y", 1, 2, 1, 1), ("y", 2, 1, 0, 2), ("zy", 2, 1, 0), ("z", 0, 1, 3),
    ("z", 0, 2, 0), ("z", 3, 2, 0), ("z", 3, 1, 4), ("yz", 3, 1, 0), ("y", 2, 2, 0, 1), ("zy", 1, 1, 1),
    ("zy", 1, 0, 2), ("yz", 0, 0, 1), ("y", 2, 2, 1, 1), ("yz", 3, 0, 2), ("zy", 2, 0, 2), ("zy", 2, 1, 1),
    ("z", 0, 1, 4), ("yz", 0, 1, 0), ("y", 1, 2, 0, 1), ("z", 0, 2, 1), ("yz", 3, 1, 1), ("z", 3, 2, 1),
    ("yz", 0, 0, 2), ("y", 1, 2, 1, 2), ("yz", 0, 1, 1), ("zy", 1, 1, 2), ("zy", 1, 0, 3), ("y", 2, 2, 0, 2),
    ("yz", 3, 1, 2), ("zy", 2, 0, 3), ("zy", 2, 1, 2), ("z", 0, 2, 2), ("y", 2, 2, 1, 2), ("zy", 2, 2, 0),
    ("yz", 0, 1, 2), ("y", 1, 2, 0, 2), ("zy", 1, 2, 0), ("z", 3, 2, 2), ("zy", 1, 0, 4), ("zy", 1, 1, 3),
    ("zy", 2, 0, 4), ("zy", 2, 1, 3), ("z", 0, 2, 3), ("zy", 2, 2, 1), ("zy", 1, 2, 1), ("z", 3, 2, 3),
    ("zy", 1, 1, 4), ("zy", 2, 1, 4), ("turn",), ("z", 0, 2, 4), ("yz", 0, 2, 0), ("zy", 2, 2, 2),
    ("zy", 1, 2, 2), ("z", 3, 2, 4), ("yz", 3, 2, 0), ("yz", 0, 2, 1), ("zy", 2, 2, 3), ("zy", 1, 2, 3),
    ("yz", 3, 2, 1), ("yz", 0, 2, 2), ("yz", 3, 2, 2), ("zy", 2, 2, 4), ("zy", 1, 2, 4),
)
ROWS = 136
F32 = jnp.float32
BF16 = jnp.bfloat16


def kernel(
    in_ref, mask_ref, rate_ref, out_ref,
    a_ref, R, LO, W, LTh, LTl, RH, RL, D, RSQ, YR, YRz, ZRy, ZRz, CF, TB,
    ag_r, rel_r, lo_r, m_r, yr_r, yz_r, zy_r, zz_r, tb_r, f_r,
    own_s, rel_s, sib_s, lo_s, m_s, yr_s, yz_s, zy_s, zz_s, tb_s, f_s, in_s,
):
    x, zh, y, zl, c = (lax.axis_index(a) for a in AXES)
    z = zh * 4 + zl
    oc = 1 - c

    def dev(dx=0, dy=0, dz=0, core=None):
        zz = (z + dz + 8) % 8
        return ((x + dx) % 4, zz // 4, (y + dy) % 4, zz % 4, c if core is None else core)

    def remote(src, dst, ss, rs, to):
        return pltpu.make_async_remote_copy(
            src_ref=src, dst_ref=dst, send_sem=ss, recv_sem=rs, device_id=to, device_id_type=MESH
        )

    def send(src, dst, ss, rs, to):
        remote(src, dst, ss, rs, to).start()

    def arrived(dst, rs):
        remote(dst, dst, f_s, rs, dev(core=oc)).wait_recv()

    def all_sent(ref, ss):
        remote(ref, ref, ss, f_r, dev(core=oc)).wait_send()

    load = pltpu.make_async_copy(in_ref, a_ref, in_s)
    load.start()

    def slot(dx, cs):
        return PLACE[dx] * 2 + cs

    lane_row = lax.broadcasted_iota(jnp.int32, (8, 128), 0)
    weights = jnp.zeros((8, 128), F32)
    for b in range(8):
        weights = jnp.where(lane_row == b, mask_ref[0, b].astype(F32), weights)
    W[slot(0, c)] = weights
    w_ref = W.at[slot(0, c)]

    partners = [dev(dx=d, core=k) for d in (1, 2, 3) for k in (0, 1)] + [dev(core=oc)]
    partners += [dev(dy=1), dev(dy=3), dev(dz=1), dev(dz=7)]
    bar = pltpu.get_barrier_semaphore()
    for p in partners:
        pl.semaphore_signal(bar, inc=1, device_id=p, device_id_type=MESH)
    pl.semaphore_wait(bar, len(partners))
    kqs = [(y + off - x + 4) % 4 for off in OFFS]
    own = kqs[3]
    takers = [((x + 1) % 4, c, (y + 3) % 4, g, zh) for g in range(4)]
    load.wait()

    def cols(q, parity, r):
        return pl.ds(pl.multiple_of((2 * q + parity) * 512 + r * 128, 128), 128)

    def rows_at(dx, cs, half=None):
        first = slot(dx, cs) * 128 + (64 if half == 1 else 0)
        return pl.ds(pl.multiple_of(first, 64), 128 if half is None else 64)

    def half_rows(half):
        return pl.ds(64 if half == 1 else 0, 128 if half is None else 64)

    def own_part(r, kq, d, half):
        for k in (0, 1):
            q = (x + d + kq) % 4
            send(a_ref.at[half_rows(half), cols(q, k, r)], R.at[kq, r, rows_at(4 - d, c, half), :],
                 own_s.at[d // 2], ag_r.at[r, 4 - d, c, kq, half or 0], dev(dx=d, core=k))

    def own_send(r, kq):
        own_part(r, kq, 1, 1)
        own_part(r, kq + 1, 1, 0)
        own_part(r, kq, 3, None)
        sibling_send(r, kq)

    def sibling_send(r, kq):
        send(a_ref.at[:, cols((x + kq) % 4, oc, r)], R.at[kq, r, rows_at(0, c), :],
             sib_s, ag_r.at[r, 0, c, kq, 0], dev(core=oc))

    def wait_part(r, dx, cs, kq, half):
        arrived(R.at[kq, r, rows_at(dx, cs, half), :], ag_r.at[r, dx, cs, kq, half or 0])

    def relay(r, kq):
        for cs in (0, 1):
            send(R.at[(kq + 1) % 4, r, rows_at(3, cs, 0), :], R.at[kq, r, rows_at(2, cs, 0), :],
                 rel_s.at[0], rel_r.at[r, 0, cs, kq], dev(dx=1))
            send(R.at[(kq + 3) % 4, r, rows_at(1, cs, 1), :], R.at[kq, r, rows_at(2, cs, 1), :],
                 rel_s.at[1], rel_r.at[r, 1, cs, kq], dev(dx=3))

    def wait_relayed(r, kq):
        for cs in (0, 1):
            for h in (0, 1):
                arrived(R.at[kq, r, rows_at(2, cs, h), :], rel_r.at[r, h, cs, kq])

    def wait_neighbours(r, kq):
        for cs in (0, 1):
            wait_part(r, 3, cs, kq, 1)
            wait_part(r, 3, cs, kq + 1, 0)
            wait_part(r, 1, cs, kq, None)

    def wait_rest(r, kq):
        wait_part(r, 0, oc, kq, None)
        wait_relayed(r, kq)

    units = [u for group in GROUPS for u in group]
    sent = [0]

    def own_sends(upto):
        for u in units[sent[0] : upto]:
            own_send(*u)
        sent[0] = max(sent[0], upto)

    def pass_on(i):
        for u in GROUPS[i]:
            wait_neighbours(*u)
        for u in GROUPS[i]:
            relay(*u)
        own_sends(sum(len(group) for group in GROUPS[: i + 2]) + AHEAD)

    for d in (1, 2, 3):
        for k in (0, 1):
            send(w_ref, W.at[slot(4 - d, c)], m_s.at[d * 2 + k], m_r.at[4 - d, c], dev(dx=d, core=k))
    send(w_ref, W.at[slot(0, c)], m_s.at[0], m_r.at[0, c], dev(core=oc))
    for r in range(4):
        own_part(r, 1, 1, 0)
        own_part(r, 3, 3, 1)
    for r in range(4):
        own_part(r, 0, 1, None)
        own_part(r, 0, 3, None)
        sibling_send(r, 0)

    for r in range(4):
        for kq in range(3):
            R[kq, r, rows_at(0, c), :] = a_ref[:, cols((x + kq) % 4, c, r)]

    for r in range(4):
        for cs in (0, 1):
            wait_part(r, 3, cs, 1, 0)
            wait_part(r, 1, cs, 3, 1)
        relay(r, 0)
    own_sends(len(GROUPS[0]) + AHEAD)

    def left(src, r, parity, first, last):
        block = 2 * x + parity
        at = pl.ds(pl.multiple_of(parity * 512 + r * 128, 128), 128)

        def step(k, squares):
            rows = pl.ds(pl.multiple_of(k * 128, 128), 128)
            raw = src[rows, :]
            turned = (raw * W[k, pl.ds(block, 1), :]).T
            high = turned.astype(BF16)
            LTh[at, rows] = high
            LTl[at, rows] = (turned - high.astype(F32)).astype(BF16)
            return squares + jnp.sum(raw * raw, axis=0, keepdims=True)

        before = RSQ[parity * 4 + r] if first else jnp.zeros((1, 128), F32)
        RSQ[parity * 4 + r] = lax.fori_loop(first, last, step, before)

    for r in range(4):
        wait_part(r, 0, oc, 0, None)
        for cs in (0, 1):
            wait_part(r, 1, cs, 0, None)
            wait_part(r, 3, cs, 0, None)
        send(R.at[0, r, 0:768], LO.at[r, 0:768], lo_s, lo_r.at[r, 0], dev(core=oc))
    arrived(W.at[slot(0, oc)], m_r.at[0, oc])
    for dx in (1, 2, 3):
        for cs in (0, 1):
            arrived(W.at[slot(dx, cs)], m_r.at[dx, cs])
    for r in range(4):
        left(R.at[0, r], r, c, 0, 6)
        arrived(LO.at[r, 0:768], lo_r.at[r, 0])
        left(LO.at[r], r, oc, 0, 6)
    for r in range(4):
        wait_relayed(r, 0)
        send(R.at[0, r, 768:1024], LO.at[r, 768:1024], lo_s, lo_r.at[r, 1], dev(core=oc))
        left(R.at[0, r], r, c, 6, 8)
    for r in range(4):
        arrived(LO.at[r, 768:1024], lo_r.at[r, 1])
        left(LO.at[r], r, oc, 6, 8)

    def product(*units):
        width = 128 * len(units)
        squares = []
        for j, (r, kq) in enumerate(units):
            src = R.at[kq, r]
            block = 2 * ((x + kq) % 4) + c
            at = slice(j * 128, j * 128 + 128)

            def split(i, total):
                rows = pl.ds(pl.multiple_of(i * 128, 128), 128)
                raw = src[rows, :]
                part = raw * W[i, pl.ds(block, 1), :]
                high = part.astype(BF16)
                RH[rows, at] = high
                RL[rows, at] = (part - high.astype(F32)).astype(BF16)
                return total + jnp.sum(raw * raw, axis=0, keepdims=True)

            squares.append(lax.fori_loop(0, 8, split, jnp.zeros((1, 128), F32)))

        def rows_of(m, carry):
            at = pl.ds(pl.multiple_of(m * 512, 512), 512)
            lh = LTh[at, :]
            rh = RH[:, 0:width]
            acc = jnp.dot(lh, rh, preferred_element_type=F32)
            acc += jnp.dot(LTl[at, :], rh, preferred_element_type=F32)
            acc += jnp.dot(lh, RL[:, 0:width], preferred_element_type=F32)
            for i in range(4):
                zd = 4 * m + i
                for j, (r, kq) in enumerate(units):
                    D[r, kq, zd, 0:128, :] = acc[i * 128 : i * 128 + 128, j * 128 : j * 128 + 128]
                    extra = jnp.where(lane_row == 0, squares[j], 0.0)
                    D[r, kq, zd, 128:ROWS, :] = jnp.where(lane_row == 1, RSQ[zd], extra)
            return carry

        lax.fori_loop(0, 2, rows_of, 0)

    def z_chain(chunk, buf, rs, ss, turn):
        def go(zd, j, way):
            send(chunk((z + zd * turn + 8) % 8), buf.at[j], ss, rs.at[j], dev(dz=way * turn))

        def take(j, zd):
            arrived(buf.at[j], rs.at[j])
            ref = chunk((z + zd * turn + 8) % 8)
            ref[...] += buf[j]

        def start():
            go(4, 0, 1)
            go(-3, 4, -1)

        def step1():
            take(0, 3)
            go(3, 1, 1)
            take(4, -2)
            go(-2, 5, -1)

        def step2():
            take(1, 2)
            go(2, 2, 1)
            take(5, -1)
            go(-1, 6, -1)

        def step3():
            take(2, 1)
            go(1, 3, 1)
            take(6, 0)

        def finish():
            take(3, 0)

        return start, step1, step2, step3, finish

    def y_chain(kq, ref, buf, rs, ss, turn):
        near, far = (1, 2) if turn == 1 else (2, 1)

        def go(j, way):
            send(ref, buf.at[j], ss.at[j], rs.at[j], dev(dy=(way * turn) % 4))

        def take(j):
            arrived(buf.at[j], rs.at[j])
            ref[...] += buf[j]

        def begin():
            @pl.when(kqs[0] == kq)
            def _():
                go(0, 1)

            @pl.when(kqs[far] == kq)
            def _():
                go(2, -1)

        def forward():
            @pl.when(kqs[near] == kq)
            def _():
                take(0)
                go(1, 1)

        def finish():
            @pl.when(own == kq)
            def _():
                take(2)
                take(1)

        return begin, forward, finish

    def y_sent(buf, ss, turn):
        for k, j in ((0, 0), (1, 1 if turn == 1 else 2), (2, 2 if turn == 1 else 1)):

            @pl.when(kqs[k] != 3)
            def _():
                all_sent(buf.at[j], ss.at[j])

    def zz(r, kq):
        i = r // 3
        return z_chain(lambda zd: D.at[r, kq, zd], ZRz.at[i, kq], zz_r.at[i, kq], zz_s.at[i, kq],
                       1 - 2 * ((kq + i) % 2))

    def zy(r, kq):
        i = r - 1
        return z_chain(lambda zd: D.at[r, kq, zd], ZRy.at[i], zy_r.at[i], zy_s.at[i], 1 - 2 * (r % 2 == 0))

    def yy(r, kq, t):
        i = r - 1
        return y_chain(kq, D.at[r, kq, t * 4 : t * 4 + 4], YR.at[i, t], yr_r.at[i, t], yr_s.at[i, t],
                       1 - 2 * t)

    def yz(r, kq):
        i = r // 3
        return y_chain(kq, D.at[r, kq, z], YRz.at[i], yz_r.at[i], yz_s.at[i], 1 - 2 * i)

    def cosines():
        row_rate = rate_ref[2 * x + z // 4]
        col_rate = rate_ref[2 * y + c]
        row_scale = row_rate * jnp.sqrt(D[0, own, z, 129:130, :] + EPS)
        row_scale = jnp.broadcast_to(row_scale, (128, 128)).T
        for r in range(4):
            col_scale = col_rate * jnp.sqrt(D[r, own, z, 128:129, :] + EPS)
            CF[:, r * 128 : r * 128 + 128] = D[r, own, z, 0:128, :] / (row_scale * col_scale)

    for name, *key in SCHEDULE:
        if name == "mul":
            for u in key:
                if u[1]:
                    wait_rest(*u)
            product(*key)
        elif name == "pass":
            pass_on(*key)
        elif name == "z":
            zz(*key[:2])[key[2]]()
        elif name == "yz":
            yz(*key[:2])[key[2]]()
        elif name == "y":
            yy(*key[:3])[key[3]]()
        elif name == "zy":

            @pl.when(own == key[1])
            def _():
                zy(*key[:2])[key[2]]()

        else:

            @pl.when(own == 1)
            def _():
                cosines()
                for g in range(4):
                    send(CF.at[:, g * 128 : g * 128 + 128], TB.at[zl], tb_s.at[g], tb_r.at[zl], takers[g])

    @pl.when((own == 0) | (own == 2))
    def _():
        cosines()

    @pl.when(own == 3)
    def _():
        for g in range(4):
            arrived(TB.at[g], tb_r.at[g])
            CF[:, g * 128 : g * 128 + 128] = TB[g].T

    half = pl.ds(pl.multiple_of(oc * 64, 64), 64)
    send(CF.at[half, :], out_ref.at[c], f_s, f_r, dev(core=oc))
    out_ref[c] = CF[pl.ds(pl.multiple_of(c * 64, 64), 64), :]
    arrived(out_ref.at[oc], f_r)
    all_sent(CF.at[half, :], f_s)
    for i in range(2):
        all_sent(a_ref.at[:, 0:3584], own_s.at[i])
        all_sent(a_ref.at[:, 0:1536], rel_s.at[i])
        y_sent(YRz.at[i], yz_s.at[i], 1 - 2 * i)
        for t in range(2):
            y_sent(YR.at[i, t], yr_s.at[i, t], 1 - 2 * t)
        for kq in range(3):
            all_sent(ZRz.at[i, kq], zz_s.at[i, kq])

        @pl.when(own != 3)
        def _():
            all_sent(ZRy.at[i], zy_s.at[i])

    @pl.when(own == 1)
    def _():
        for g in range(4):
            all_sent(TB.at[g], tb_s.at[g])

    all_sent(a_ref.at[:, 0:1536], sib_s)
    all_sent(LO, lo_s)
    for i in [0] + list(range(2, 8)):
        all_sent(w_ref, m_s.at[i])


def per_device(samples, keep_mask, keep_rate):
    dma = pltpu.SemaphoreType.DMA
    vmem = pltpu.VMEM
    return pl.pallas_call(
        kernel,
        out_shape=jax.ShapeDtypeStruct((2, 64, 512), F32),
        in_specs=[
            pl.BlockSpec(memory_space=pl.ANY),
            pl.BlockSpec(memory_space=pltpu.SMEM),
            pl.BlockSpec(memory_space=pltpu.SMEM),
        ],
        out_specs=pl.BlockSpec(memory_space=pltpu.VMEM),
        scratch_shapes=[
            vmem((128, 4096), F32),
            vmem((4, 4, 1024, 128), F32),
            vmem((4, 1024, 128), F32),
            vmem((8, 8, 128), F32),
            vmem((1024, 1024), BF16),
            vmem((1024, 1024), BF16),
            vmem((1024, 256), BF16),
            vmem((1024, 256), BF16),
            vmem((4, 4, 8, ROWS, 128), F32),
            vmem((8, 1, 128), F32),
            vmem((2, 2, 3, 4, ROWS, 128), F32),
            vmem((2, 3, ROWS, 128), F32),
            vmem((2, 7, ROWS, 128), F32),
            vmem((2, 3, 7, ROWS, 128), F32),
            vmem((128, 512), F32),
            vmem((4, 128, 128), F32),
            dma((4, 4, 2, 4, 2)),
            dma((4, 2, 2, 4)),
            dma((4, 2)),
            dma((4, 2)),
            dma((2, 2, 3)),
            dma((2, 3)),
            dma((2, 7)),
            dma((2, 3, 7)),
            dma((4,)),
            dma,
            dma((2,)),
            dma((2,)),
            dma,
            dma,
            dma((8,)),
            dma((2, 2, 3)),
            dma((2, 3)),
            dma((2,)),
            dma((2, 3)),
            dma((4,)),
            dma,
            dma,
        ],
        compiler_params=pltpu.CompilerParams(
            collective_id=0, has_side_effects=True, vmem_limit_bytes=60 << 20
        ),
        name="sampled_gram",
    )(samples, keep_mask, keep_rate)


def solution(mesh):
    finer = Mesh(mesh.devices.reshape(4, 2, 4, 4, 2), AXES)
    rows = P(AXES, None)
    return jax.shard_map(
        per_device,
        mesh=finer,
        in_specs=(rows, rows, P()),
        out_specs=P(("x", "zh", "y"), ("zl", "c"), None),
        check_vma=False,
    )
```

```python
import jax
import jax.numpy as jnp
from jax import lax
from jax.experimental import pallas as pl
from jax.experimental.pallas import tpu as pltpu
from jax.sharding import Mesh
from jax.sharding import PartitionSpec as P

AXES = ("x", "zh", "y", "zl", "c")
EPS = 1e-06
MESH = pl.DeviceIdType.MESH
OFFS = (2, 1, 3, 0)
PLACE = {0: 0, 1: 1, 3: 2, 2: 3}
GROUPS = (((1, 1), (2, 1)), ((0, 1), (3, 1)), ((1, 2), (2, 2)), ((0, 2), (3, 2)))
AHEAD = 1
SCHEDULE = (
    ("mul", (0, 0), (3, 0)), ("pass", 0), ("mul", (1, 0), (2, 0)), ("z", 0, 0, 0), ("y", 2, 0, 0, 0),
    ("y", 1, 0, 1, 0), ("mul", (1, 1), (2, 1)), ("y", 2, 1, 1, 0), ("z", 0, 0, 1), ("y", 1, 1, 0, 0),
    ("pass", 1), ("y", 2, 1, 0, 0), ("z", 3, 0, 0), ("z", 3, 0, 1), ("y", 1, 1, 1, 0), ("z", 0, 0, 2),
    ("mul", (0, 1), (3, 1)), ("pass", 2), ("z", 0, 1, 0), ("z", 3, 1, 0), ("z", 3, 0, 2), ("y", 2, 0, 1, 0),
    ("y", 1, 1, 0, 1), ("y", 1, 0, 1, 1), ("z", 0, 1, 1), ("mul", (1, 2), (2, 2)), ("z", 3, 1, 1),
    ("y", 2, 2, 0, 0), ("z", 0, 0, 3), ("y", 2, 0, 0, 1), ("y", 1, 0, 0, 0), ("y", 2, 1, 0, 1),
    ("y", 2, 2, 1, 0), ("pass", 3), ("y", 1, 2, 1, 0), ("z", 0, 1, 2), ("y", 1, 1, 1, 1), ("y", 1, 2, 0, 0),
    ("y", 2, 1, 1, 1), ("y", 1, 1, 0, 2), ("z", 3, 0, 3), ("z", 3, 1, 2), ("mul", (0, 2), (3, 2)),
    ("y", 2, 0, 1, 1), ("y", 2, 2, 1, 1), ("z", 3, 2, 0), ("y", 2, 2, 0, 1), ("z", 0, 2, 0), ("z", 3, 0, 4),
    ("y", 1, 1, 1, 2), ("zy", 1, 1, 0), ("z", 0, 1, 3), ("y", 1, 0, 0, 1), ("z", 3, 1, 3), ("y", 1, 2, 1, 1),
    ("z", 3, 2, 1), ("zy", 1, 1, 1), ("y", 2, 1, 0, 2), ("y", 2, 0, 0, 2), ("z", 0, 0, 4), ("z", 0, 2, 1),
    ("y", 2, 1, 1, 2), ("yz", 0, 0, 0), ("y", 1, 0, 1, 2), ("zy", 2, 1, 0), ("y", 2, 0, 1, 2), ("z", 3, 2, 2),
    ("z", 0, 1, 4), ("y", 1, 0, 0, 2), ("zy", 2, 0, 0), ("y", 2, 2, 0, 2), ("y", 1, 2, 0, 1), ("z", 0, 2, 2),
    ("yz", 0, 0, 1), ("zy", 2, 1, 1), ("z", 3, 1, 4), ("yz", 3, 0, 0), ("zy", 1, 0, 0), ("zy", 1, 1, 2),
    ("zy", 2, 1, 2), ("y", 2, 2, 1, 2), ("zy", 2, 2, 0), ("y", 1, 2, 1, 2), ("yz", 3, 1, 0), ("z", 3, 2, 3),
    ("zy", 2, 2, 1), ("z", 0, 2, 3), ("yz", 3, 0, 1), ("zy", 2, 1, 3), ("y", 1, 2, 0, 2), ("zy", 2, 0, 1),
    ("zy", 1, 1, 3), ("zy", 1, 2, 0), ("yz", 0, 1, 0), ("yz", 3, 1, 1), ("yz", 3, 1, 2), ("z", 3, 2, 4),
    ("zy", 1, 1, 4), ("zy", 1, 2, 1), ("zy", 1, 0, 1), ("yz", 0, 1, 1), ("yz", 0, 1, 2), ("zy", 2, 1, 4),
    ("yz", 3, 2, 0), ("z", 0, 2, 4), ("yz", 0, 2, 0), ("yz", 0, 0, 2), ("yz", 3, 2, 1), ("zy", 2, 0, 2),
    ("zy", 2, 2, 2), ("turn",), ("zy", 1, 0, 2), ("zy", 1, 2, 2), ("zy", 2, 2, 3), ("zy", 1, 2, 3),
    ("zy", 1, 0, 3), ("yz", 3, 2, 2), ("yz", 3, 0, 2), ("yz", 0, 2, 1), ("zy", 2, 2, 4), ("yz", 0, 2, 2),
    ("zy", 2, 0, 3), ("zy", 2, 0, 4), ("zy", 1, 2, 4), ("zy", 1, 0, 4),
)
ROWS = 136
F32 = jnp.float32
BF16 = jnp.bfloat16


def kernel(
    in_ref, mask_ref, rate_ref, out_ref,
    a_ref, R, LO, W, LTh, LTl, RH, RL, D, RSQ, YR, YRz, ZRy, ZRz, CF, TB,
    ag_r, rel_r, lo_r, m_r, yr_r, yz_r, zy_r, zz_r, tb_r, f_r,
    own_s, rel_s, sib_s, lo_s, m_s, yr_s, yz_s, zy_s, zz_s, tb_s, f_s, in_s,
):
    x, zh, y, zl, c = (lax.axis_index(a) for a in AXES)
    z = zh * 4 + zl
    oc = 1 - c

    def dev(dx=0, dy=0, dz=0, core=None):
        zz = (z + dz + 8) % 8
        return ((x + dx) % 4, zz // 4, (y + dy) % 4, zz % 4, c if core is None else core)

    def remote(src, dst, ss, rs, to):
        return pltpu.make_async_remote_copy(
            src_ref=src, dst_ref=dst, send_sem=ss, recv_sem=rs, device_id=to, device_id_type=MESH
        )

    def send(src, dst, ss, rs, to):
        remote(src, dst, ss, rs, to).start()

    def arrived(dst, rs):
        remote(dst, dst, f_s, rs, dev(core=oc)).wait_recv()

    def all_sent(ref, ss):
        remote(ref, ref, ss, f_r, dev(core=oc)).wait_send()

    load = pltpu.make_async_copy(in_ref, a_ref, in_s)
    load.start()

    def slot(dx, cs):
        return PLACE[dx] * 2 + cs

    lane_row = lax.broadcasted_iota(jnp.int32, (8, 128), 0)
    weights = jnp.zeros((8, 128), F32)
    for b in range(8):
        weights = jnp.where(lane_row == b, mask_ref[0, b].astype(F32), weights)
    W[slot(0, c)] = weights
    w_ref = W.at[slot(0, c)]

    partners = [dev(dx=d, core=k) for d in (1, 2, 3) for k in (0, 1)] + [dev(core=oc)]
    partners += [dev(dy=1), dev(dy=3), dev(dz=1), dev(dz=7)]
    bar = pltpu.get_barrier_semaphore()
    for p in partners:
        pl.semaphore_signal(bar, inc=1, device_id=p, device_id_type=MESH)
    pl.semaphore_wait(bar, len(partners))
    kqs = [(y + off - x + 4) % 4 for off in OFFS]
    own = kqs[3]
    takers = [((x + 1) % 4, c, (y + 3) % 4, g, zh) for g in range(4)]
    load.wait()

    def cols(q, parity, r):
        return pl.ds(pl.multiple_of((2 * q + parity) * 512 + r * 128, 128), 128)

    def rows_at(dx, cs, half=None):
        first = slot(dx, cs) * 128 + (64 if half == 1 else 0)
        return pl.ds(pl.multiple_of(first, 64), 128 if half is None else 64)

    def half_rows(half):
        return pl.ds(64 if half == 1 else 0, 128 if half is None else 64)

    def own_part(r, kq, d, half):
        for k in (0, 1):
            q = (x + d + kq) % 4
            send(a_ref.at[half_rows(half), cols(q, k, r)], R.at[kq, r, rows_at(4 - d, c, half), :],
                 own_s.at[d // 2], ag_r.at[r, 4 - d, c, kq, half or 0], dev(dx=d, core=k))

    def own_send(r, kq):
        own_part(r, kq, 1, 1)
        own_part(r, kq + 1, 1, 0)
        own_part(r, kq, 3, None)
        sibling_send(r, kq)

    def sibling_send(r, kq):
        send(a_ref.at[:, cols((x + kq) % 4, oc, r)], R.at[kq, r, rows_at(0, c), :],
             sib_s, ag_r.at[r, 0, c, kq, 0], dev(core=oc))

    def wait_part(r, dx, cs, kq, half):
        arrived(R.at[kq, r, rows_at(dx, cs, half), :], ag_r.at[r, dx, cs, kq, half or 0])

    def relay(r, kq):
        for cs in (0, 1):
            send(R.at[(kq + 1) % 4, r, rows_at(3, cs, 0), :], R.at[kq, r, rows_at(2, cs, 0), :],
                 rel_s.at[0], rel_r.at[r, 0, cs, kq], dev(dx=1))
            send(R.at[(kq + 3) % 4, r, rows_at(1, cs, 1), :], R.at[kq, r, rows_at(2, cs, 1), :],
                 rel_s.at[1], rel_r.at[r, 1, cs, kq], dev(dx=3))

    def wait_relayed(r, kq):
        for cs in (0, 1):
            for h in (0, 1):
                arrived(R.at[kq, r, rows_at(2, cs, h), :], rel_r.at[r, h, cs, kq])

    def wait_neighbours(r, kq):
        for cs in (0, 1):
            wait_part(r, 3, cs, kq, 1)
            wait_part(r, 3, cs, kq + 1, 0)
            wait_part(r, 1, cs, kq, None)

    def wait_rest(r, kq):
        wait_part(r, 0, oc, kq, None)
        wait_relayed(r, kq)

    units = [u for group in GROUPS for u in group]
    sent = [0]

    def own_sends(upto):
        for u in units[sent[0] : upto]:
            own_send(*u)
        sent[0] = max(sent[0], upto)

    def pass_on(i):
        for u in GROUPS[i]:
            wait_neighbours(*u)
        for u in GROUPS[i]:
            relay(*u)
        own_sends(sum(len(group) for group in GROUPS[: i + 2]) + AHEAD)

    for d in (1, 2, 3):
        for k in (0, 1):
            send(w_ref, W.at[slot(4 - d, c)], m_s.at[d * 2 + k], m_r.at[4 - d, c], dev(dx=d, core=k))
    send(w_ref, W.at[slot(0, c)], m_s.at[0], m_r.at[0, c], dev(core=oc))
    for r in range(4):
        own_part(r, 1, 1, 0)
        own_part(r, 3, 3, 1)
    for r in range(4):
        own_part(r, 0, 1, None)
        own_part(r, 0, 3, None)
        sibling_send(r, 0)

    for r in range(4):
        for kq in range(3):
            R[kq, r, rows_at(0, c), :] = a_ref[:, cols((x + kq) % 4, c, r)]

    for r in range(4):
        for cs in (0, 1):
            wait_part(r, 3, cs, 1, 0)
            wait_part(r, 1, cs, 3, 1)
        relay(r, 0)
    own_sends(len(GROUPS[0]) + AHEAD)

    def left(src, r, parity, first, last):
        block = 2 * x + parity
        at = pl.ds(pl.multiple_of(parity * 512 + r * 128, 128), 128)

        def step(k, squares):
            rows = pl.ds(pl.multiple_of(k * 128, 128), 128)
            raw = src[rows, :]
            turned = (raw * W[k, pl.ds(block, 1), :]).T
            high = turned.astype(BF16)
            LTh[at, rows] = high
            LTl[at, rows] = (turned - high.astype(F32)).astype(BF16)
            return squares + jnp.sum(raw * raw, axis=0, keepdims=True)

        before = RSQ[parity * 4 + r] if first else jnp.zeros((1, 128), F32)
        RSQ[parity * 4 + r] = lax.fori_loop(first, last, step, before)

    for r in range(4):
        wait_part(r, 0, oc, 0, None)
        for cs in (0, 1):
            wait_part(r, 1, cs, 0, None)
            wait_part(r, 3, cs, 0, None)
        send(R.at[0, r, 0:768], LO.at[r, 0:768], lo_s, lo_r.at[r, 0], dev(core=oc))
    arrived(W.at[slot(0, oc)], m_r.at[0, oc])
    for dx in (1, 2, 3):
        for cs in (0, 1):
            arrived(W.at[slot(dx, cs)], m_r.at[dx, cs])
    for r in range(4):
        left(R.at[0, r], r, c, 0, 6)
        arrived(LO.at[r, 0:768], lo_r.at[r, 0])
        left(LO.at[r], r, oc, 0, 6)
    for r in range(4):
        wait_relayed(r, 0)
        send(R.at[0, r, 768:1024], LO.at[r, 768:1024], lo_s, lo_r.at[r, 1], dev(core=oc))
        left(R.at[0, r], r, c, 6, 8)
    for r in range(4):
        arrived(LO.at[r, 768:1024], lo_r.at[r, 1])
        left(LO.at[r], r, oc, 6, 8)

    def product(*units):
        width = 128 * len(units)
        squares = []
        for j, (r, kq) in enumerate(units):
            src = R.at[kq, r]
            block = 2 * ((x + kq) % 4) + c
            at = slice(j * 128, j * 128 + 128)

            def split(i, total):
                rows = pl.ds(pl.multiple_of(i * 128, 128), 128)
                raw = src[rows, :]
                part = raw * W[i, pl.ds(block, 1), :]
                high = part.astype(BF16)
                RH[rows, at] = high
                RL[rows, at] = (part - high.astype(F32)).astype(BF16)
                return total + jnp.sum(raw * raw, axis=0, keepdims=True)

            squares.append(lax.fori_loop(0, 8, split, jnp.zeros((1, 128), F32)))

        def rows_of(m, carry):
            at = pl.ds(pl.multiple_of(m * 512, 512), 512)
            lh = LTh[at, :]
            rh = RH[:, 0:width]
            acc = jnp.dot(lh, rh, preferred_element_type=F32)
            acc += jnp.dot(LTl[at, :], rh, preferred_element_type=F32)
            acc += jnp.dot(lh, RL[:, 0:width], preferred_element_type=F32)
            for i in range(4):
                zd = 4 * m + i
                for j, (r, kq) in enumerate(units):
                    D[r, kq, zd, 0:128, :] = acc[i * 128 : i * 128 + 128, j * 128 : j * 128 + 128]
                    extra = jnp.where(lane_row == 0, squares[j], 0.0)
                    D[r, kq, zd, 128:ROWS, :] = jnp.where(lane_row == 1, RSQ[zd], extra)
            return carry

        lax.fori_loop(0, 2, rows_of, 0)

    def z_chain(chunk, buf, rs, ss, turn):
        def go(zd, j, way):
            send(chunk((z + zd * turn + 8) % 8), buf.at[j], ss, rs.at[j], dev(dz=way * turn))

        def take(j, zd):
            arrived(buf.at[j], rs.at[j])
            ref = chunk((z + zd * turn + 8) % 8)
            ref[...] += buf[j]

        def start():
            go(4, 0, 1)
            go(-3, 4, -1)

        def step1():
            take(0, 3)
            go(3, 1, 1)
            take(4, -2)
            go(-2, 5, -1)

        def step2():
            take(1, 2)
            go(2, 2, 1)
            take(5, -1)
            go(-1, 6, -1)

        def step3():
            take(2, 1)
            go(1, 3, 1)
            take(6, 0)

        def finish():
            take(3, 0)

        return start, step1, step2, step3, finish

    def y_chain(kq, ref, buf, rs, ss, turn):
        near, far = (1, 2) if turn == 1 else (2, 1)

        def go(j, way):
            send(ref, buf.at[j], ss.at[j], rs.at[j], dev(dy=(way * turn) % 4))

        def take(j):
            arrived(buf.at[j], rs.at[j])
            ref[...] += buf[j]

        def begin():
            @pl.when(kqs[0] == kq)
            def _():
                go(0, 1)

            @pl.when(kqs[far] == kq)
            def _():
                go(2, -1)

        def forward():
            @pl.when(kqs[near] == kq)
            def _():
                take(0)
                go(1, 1)

        def finish():
            @pl.when(own == kq)
            def _():
                take(2)
                take(1)

        return begin, forward, finish

    def y_sent(buf, ss, turn):
        for k, j in ((0, 0), (1, 1 if turn == 1 else 2), (2, 2 if turn == 1 else 1)):

            @pl.when(kqs[k] != 3)
            def _():
                all_sent(buf.at[j], ss.at[j])

    def zz(r, kq):
        i = r // 3
        return z_chain(lambda zd: D.at[r, kq, zd], ZRz.at[i, kq], zz_r.at[i, kq], zz_s.at[i, kq],
                       1 - 2 * ((kq + i) % 2))

    def zy(r, kq):
        i = r - 1
        return z_chain(lambda zd: D.at[r, kq, zd], ZRy.at[i], zy_r.at[i], zy_s.at[i], 1 - 2 * (r % 2 == 0))

    def yy(r, kq, t):
        i = r - 1
        return y_chain(kq, D.at[r, kq, t * 4 : t * 4 + 4], YR.at[i, t], yr_r.at[i, t], yr_s.at[i, t],
                       1 - 2 * t)

    def yz(r, kq):
        i = r // 3
        return y_chain(kq, D.at[r, kq, z], YRz.at[i], yz_r.at[i], yz_s.at[i], 1 - 2 * i)

    def cosines():
        row_rate = rate_ref[2 * x + z // 4]
        col_rate = rate_ref[2 * y + c]
        row_scale = row_rate * jnp.sqrt(D[0, own, z, 129:130, :] + EPS)
        row_scale = jnp.broadcast_to(row_scale, (128, 128)).T
        for r in range(4):
            col_scale = col_rate * jnp.sqrt(D[r, own, z, 128:129, :] + EPS)
            CF[:, r * 128 : r * 128 + 128] = D[r, own, z, 0:128, :] / (row_scale * col_scale)

    for name, *key in SCHEDULE:
        if name == "mul":
            for u in key:
                if u[1]:
                    wait_rest(*u)
            product(*key)
        elif name == "pass":
            pass_on(*key)
        elif name == "z":
            zz(*key[:2])[key[2]]()
        elif name == "yz":
            yz(*key[:2])[key[2]]()
        elif name == "y":
            yy(*key[:3])[key[3]]()
        elif name == "zy":

            @pl.when(own == key[1])
            def _():
                zy(*key[:2])[key[2]]()

        else:

            @pl.when(own == 1)
            def _():
                cosines()
                for g in range(4):
                    send(CF.at[:, g * 128 : g * 128 + 128], TB.at[zl], tb_s.at[g], tb_r.at[zl], takers[g])

    @pl.when((own == 0) | (own == 2))
    def _():
        cosines()

    @pl.when(own == 3)
    def _():
        for g in range(4):
            arrived(TB.at[g], tb_r.at[g])
            CF[:, g * 128 : g * 128 + 128] = TB[g].T

    half = pl.ds(pl.multiple_of(oc * 64, 64), 64)
    send(CF.at[half, :], out_ref.at[c], f_s, f_r, dev(core=oc))
    out_ref[c] = CF[pl.ds(pl.multiple_of(c * 64, 64), 64), :]
    arrived(out_ref.at[oc], f_r)
    all_sent(CF.at[half, :], f_s)
    for i in range(2):
        all_sent(a_ref.at[:, 0:3584], own_s.at[i])
        all_sent(a_ref.at[:, 0:1536], rel_s.at[i])
        y_sent(YRz.at[i], yz_s.at[i], 1 - 2 * i)
        for t in range(2):
            y_sent(YR.at[i, t], yr_s.at[i, t], 1 - 2 * t)
        for kq in range(3):
            all_sent(ZRz.at[i, kq], zz_s.at[i, kq])

        @pl.when(own != 3)
        def _():
            all_sent(ZRy.at[i], zy_s.at[i])

    @pl.when(own == 1)
    def _():
        for g in range(4):
            all_sent(TB.at[g], tb_s.at[g])

    all_sent(a_ref.at[:, 0:1536], sib_s)
    all_sent(LO, lo_s)
    for i in [0] + list(range(2, 8)):
        all_sent(w_ref, m_s.at[i])


def per_device(samples, keep_mask, keep_rate):
    dma = pltpu.SemaphoreType.DMA
    vmem = pltpu.VMEM
    return pl.pallas_call(
        kernel,
        out_shape=jax.ShapeDtypeStruct((2, 64, 512), F32),
        in_specs=[
            pl.BlockSpec(memory_space=pl.ANY),
            pl.BlockSpec(memory_space=pltpu.SMEM),
            pl.BlockSpec(memory_space=pltpu.SMEM),
        ],
        out_specs=pl.BlockSpec(memory_space=pltpu.VMEM),
        scratch_shapes=[
            vmem((128, 4096), F32),
            vmem((4, 4, 1024, 128), F32),
            vmem((4, 1024, 128), F32),
            vmem((8, 8, 128), F32),
            vmem((1024, 1024), BF16),
            vmem((1024, 1024), BF16),
            vmem((1024, 256), BF16),
            vmem((1024, 256), BF16),
            vmem((4, 4, 8, ROWS, 128), F32),
            vmem((8, 1, 128), F32),
            vmem((2, 2, 3, 4, ROWS, 128), F32),
            vmem((2, 3, ROWS, 128), F32),
            vmem((2, 7, ROWS, 128), F32),
            vmem((2, 3, 7, ROWS, 128), F32),
            vmem((128, 512), F32),
            vmem((4, 128, 128), F32),
            dma((4, 4, 2, 4, 2)),
            dma((4, 2, 2, 4)),
            dma((4, 2)),
            dma((4, 2)),
            dma((2, 2, 3)),
            dma((2, 3)),
            dma((2, 7)),
            dma((2, 3, 7)),
            dma((4,)),
            dma,
            dma((2,)),
            dma((2,)),
            dma,
            dma,
            dma((8,)),
            dma((2, 2, 3)),
            dma((2, 3)),
            dma((2,)),
            dma((2, 3)),
            dma((4,)),
            dma,
            dma,
        ],
        compiler_params=pltpu.CompilerParams(
            collective_id=0, has_side_effects=True, vmem_limit_bytes=60 << 20
        ),
        name="sampled_gram",
    )(samples, keep_mask, keep_rate)


def solution(mesh):
    finer = Mesh(mesh.devices.reshape(4, 2, 4, 4, 2), AXES)
    rows = P(AXES, None)
    return jax.shard_map(
        per_device,
        mesh=finer,
        in_specs=(rows, rows, P()),
        out_specs=P(("x", "zh", "y"), ("zl", "c"), None),
        check_vma=False,
    )
```

```python
import jax
import jax.numpy as jnp
from jax import lax
from jax.experimental import pallas as pl
from jax.experimental.pallas import tpu as pltpu
from jax.sharding import Mesh
from jax.sharding import PartitionSpec as P

AXES = ("x", "zh", "y", "zl", "c")
EPS = 1e-06
MESH = pl.DeviceIdType.MESH
OFFS = (2, 1, 3, 0)
PLACE = {0: 0, 1: 1, 3: 2, 2: 3}
GROUPS = (((1, 1), (2, 1)), ((0, 1), (1, 2)), ((2, 2), (3, 1)), ((0, 2), (3, 2)))
AHEAD = 1
SCHEDULE = (
    ("mul", (0, 0), (3, 0)), ("z", 3, 0, 0), ("pass", 0), ("mul", (1, 0), (2, 0)), ("z", 0, 0, 0),
    ("y", 1, 0, 1, 0), ("y", 1, 0, 0, 0), ("z", 3, 0, 1), ("mul", (1, 1), (2, 1)), ("y", 1, 1, 1, 0),
    ("y", 2, 0, 0, 0), ("z", 3, 0, 2), ("y", 2, 1, 0, 0), ("z", 0, 0, 1), ("y", 2, 1, 1, 0), ("pass", 1),
    ("y", 1, 0, 1, 1), ("y", 1, 1, 0, 0), ("mul", (0, 1), (1, 2)), ("y", 1, 2, 1, 0), ("z", 0, 1, 0),
    ("z", 0, 0, 2), ("pass", 2), ("y", 2, 0, 1, 0), ("y", 1, 2, 0, 0), ("y", 2, 1, 0, 1), ("z", 0, 1, 1),
    ("mul", (2, 2), (3, 1)), ("z", 3, 1, 0), ("z", 3, 0, 3), ("y", 1, 0, 1, 2), ("y", 2, 0, 0, 1),
    ("pass", 3), ("y", 1, 2, 1, 1), ("y", 2, 2, 1, 0), ("z", 0, 0, 3), ("y", 1, 0, 0, 1), ("y", 1, 1, 1, 1),
    ("y", 1, 1, 0, 1), ("y", 2, 0, 1, 1), ("z", 3, 1, 1), ("z", 0, 1, 2), ("mul", (0, 2), (3, 2)),
    ("z", 0, 2, 0), ("z", 3, 0, 4), ("z", 0, 0, 4), ("z", 3, 2, 0), ("y", 2, 2, 0, 0), ("y", 1, 2, 0, 1),
    ("y", 2, 1, 1, 1), ("y", 2, 0, 0, 2), ("z", 3, 1, 2), ("y", 2, 1, 0, 2), ("z", 0, 2, 1), ("z", 3, 2, 1),
    ("y", 1, 1, 0, 2), ("y", 1, 1, 1, 2), ("zy", 1, 1, 0), ("y", 2, 1, 1, 2), ("z", 0, 1, 3), ("z", 3, 1, 3),
    ("y", 1, 0, 0, 2), ("y", 1, 2, 1, 2), ("zy", 1, 0, 0), ("zy", 2, 1, 0), ("y", 1, 2, 0, 2),
    ("y", 2, 2, 1, 1), ("zy", 1, 1, 1), ("y", 2, 2, 0, 1), ("yz", 0, 0, 0), ("z", 3, 2, 2), ("zy", 1, 2, 0),
    ("z", 0, 1, 4), ("yz", 0, 1, 0), ("zy", 2, 1, 1), ("z", 0, 2, 2), ("zy", 1, 1, 2), ("y", 2, 2, 1, 2),
    ("y", 2, 0, 1, 2), ("zy", 1, 0, 1), ("yz", 3, 0, 0), ("z", 3, 1, 4), ("yz", 3, 1, 0), ("zy", 2, 1, 2),
    ("z", 3, 2, 3), ("zy", 1, 2, 1), ("zy", 1, 1, 3), ("yz", 3, 0, 1), ("zy", 2, 0, 0), ("yz", 0, 0, 1),
    ("zy", 1, 0, 2), ("yz", 3, 1, 1), ("yz", 0, 1, 1), ("z", 0, 2, 3), ("yz", 3, 1, 2), ("y", 2, 2, 0, 2),
    ("zy", 2, 2, 0), ("zy", 2, 1, 3), ("zy", 2, 0, 1), ("z", 0, 2, 4), ("zy", 2, 2, 1), ("yz", 0, 2, 0),
    ("zy", 1, 2, 2), ("zy", 1, 1, 4), ("zy", 2, 2, 2), ("yz", 0, 1, 2), ("yz", 0, 0, 2), ("yz", 0, 2, 1),
    ("yz", 0, 2, 2), ("z", 3, 2, 4), ("zy", 1, 2, 3), ("zy", 2, 2, 3), ("yz", 3, 2, 0), ("yz", 3, 2, 1),
    ("zy", 2, 1, 4), ("zy", 2, 0, 2), ("zy", 1, 2, 4), ("zy", 1, 0, 3), ("zy", 2, 0, 3), ("zy", 1, 0, 4),
    ("yz", 3, 0, 2), ("zy", 2, 0, 4), ("turn",), ("yz", 3, 2, 2), ("zy", 2, 2, 4),
)
ROWS = 136
F32 = jnp.float32
BF16 = jnp.bfloat16


def kernel(
    in_ref, mask_ref, rate_ref, out_ref,
    a_ref, R, LO, W, LTh, LTl, RH, RL, D, RSQ, YR, YRz, ZRy, ZRz, CF, TB,
    ag_r, rel_r, lo_r, m_r, yr_r, yz_r, zy_r, zz_r, tb_r, f_r,
    own_s, rel_s, sib_s, lo_s, m_s, yr_s, yz_s, zy_s, zz_s, tb_s, f_s, in_s,
):
    x, zh, y, zl, c = (lax.axis_index(a) for a in AXES)
    z = zh * 4 + zl
    oc = 1 - c

    def dev(dx=0, dy=0, dz=0, core=None):
        zz = (z + dz + 8) % 8
        return ((x + dx) % 4, zz // 4, (y + dy) % 4, zz % 4, c if core is None else core)

    def remote(src, dst, ss, rs, to):
        return pltpu.make_async_remote_copy(
            src_ref=src, dst_ref=dst, send_sem=ss, recv_sem=rs, device_id=to, device_id_type=MESH
        )

    def send(src, dst, ss, rs, to):
        remote(src, dst, ss, rs, to).start()

    def arrived(dst, rs):
        remote(dst, dst, f_s, rs, dev(core=oc)).wait_recv()

    def all_sent(ref, ss):
        remote(ref, ref, ss, f_r, dev(core=oc)).wait_send()

    load = pltpu.make_async_copy(in_ref, a_ref, in_s)
    load.start()

    def slot(dx, cs):
        return PLACE[dx] * 2 + cs

    lane_row = lax.broadcasted_iota(jnp.int32, (8, 128), 0)
    weights = jnp.zeros((8, 128), F32)
    for b in range(8):
        weights = jnp.where(lane_row == b, mask_ref[0, b].astype(F32), weights)
    W[slot(0, c)] = weights
    w_ref = W.at[slot(0, c)]

    partners = [dev(dx=d, core=k) for d in (1, 2, 3) for k in (0, 1)] + [dev(core=oc)]
    partners += [dev(dy=1), dev(dy=3), dev(dz=1), dev(dz=7)]
    bar = pltpu.get_barrier_semaphore()
    for p in partners:
        pl.semaphore_signal(bar, inc=1, device_id=p, device_id_type=MESH)
    pl.semaphore_wait(bar, len(partners))
    kqs = [(y + off - x + 4) % 4 for off in OFFS]
    own = kqs[3]
    takers = [((x + 1) % 4, c, (y + 3) % 4, g, zh) for g in range(4)]
    load.wait()

    def cols(q, parity, r):
        return pl.ds(pl.multiple_of((2 * q + parity) * 512 + r * 128, 128), 128)

    def rows_at(dx, cs, half=None):
        first = slot(dx, cs) * 128 + (64 if half == 1 else 0)
        return pl.ds(pl.multiple_of(first, 64), 128 if half is None else 64)

    def half_rows(half):
        return pl.ds(64 if half == 1 else 0, 128 if half is None else 64)

    def own_part(r, kq, d, half):
        for k in (0, 1):
            q = (x + d + kq) % 4
            send(a_ref.at[half_rows(half), cols(q, k, r)], R.at[kq, r, rows_at(4 - d, c, half), :],
                 own_s.at[d // 2], ag_r.at[r, 4 - d, c, kq, half or 0], dev(dx=d, core=k))

    def own_send(r, kq):
        own_part(r, kq, 1, 1)
        own_part(r, kq + 1, 1, 0)
        own_part(r, kq, 3, None)
        sibling_send(r, kq)

    def sibling_send(r, kq):
        send(a_ref.at[:, cols((x + kq) % 4, oc, r)], R.at[kq, r, rows_at(0, c), :],
             sib_s, ag_r.at[r, 0, c, kq, 0], dev(core=oc))

    def wait_part(r, dx, cs, kq, half):
        arrived(R.at[kq, r, rows_at(dx, cs, half), :], ag_r.at[r, dx, cs, kq, half or 0])

    def relay(r, kq):
        for cs in (0, 1):
            send(R.at[(kq + 1) % 4, r, rows_at(3, cs, 0), :], R.at[kq, r, rows_at(2, cs, 0), :],
                 rel_s.at[0], rel_r.at[r, 0, cs, kq], dev(dx=1))
            send(R.at[(kq + 3) % 4, r, rows_at(1, cs, 1), :], R.at[kq, r, rows_at(2, cs, 1), :],
                 rel_s.at[1], rel_r.at[r, 1, cs, kq], dev(dx=3))

    def wait_relayed(r, kq):
        for cs in (0, 1):
            for h in (0, 1):
                arrived(R.at[kq, r, rows_at(2, cs, h), :], rel_r.at[r, h, cs, kq])

    def wait_neighbours(r, kq):
        for cs in (0, 1):
            wait_part(r, 3, cs, kq, 1)
            wait_part(r, 3, cs, kq + 1, 0)
            wait_part(r, 1, cs, kq, None)

    def wait_rest(r, kq):
        wait_part(r, 0, oc, kq, None)
        wait_relayed(r, kq)

    units = [u for group in GROUPS for u in group]
    sent = [0]

    def own_sends(upto):
        for u in units[sent[0] : upto]:
            own_send(*u)
        sent[0] = max(sent[0], upto)

    def pass_on(i):
        for u in GROUPS[i]:
            wait_neighbours(*u)
        for u in GROUPS[i]:
            relay(*u)
        own_sends(sum(len(group) for group in GROUPS[: i + 2]) + AHEAD)

    for d in (1, 2, 3):
        for k in (0, 1):
            send(w_ref, W.at[slot(4 - d, c)], m_s.at[d * 2 + k], m_r.at[4 - d, c], dev(dx=d, core=k))
    send(w_ref, W.at[slot(0, c)], m_s.at[0], m_r.at[0, c], dev(core=oc))
    for r in range(4):
        own_part(r, 1, 1, 0)
        own_part(r, 3, 3, 1)
    for r in range(4):
        own_part(r, 0, 1, None)
        own_part(r, 0, 3, None)
        sibling_send(r, 0)

    for r in range(4):
        for kq in range(3):
            R[kq, r, rows_at(0, c), :] = a_ref[:, cols((x + kq) % 4, c, r)]

    for r in range(4):
        for cs in (0, 1):
            wait_part(r, 3, cs, 1, 0)
            wait_part(r, 1, cs, 3, 1)
        relay(r, 0)
    own_sends(len(GROUPS[0]) + AHEAD)

    def left(src, r, parity, first, last):
        block = 2 * x + parity
        at = pl.ds(pl.multiple_of(parity * 512 + r * 128, 128), 128)

        def step(k, squares):
            rows = pl.ds(pl.multiple_of(k * 128, 128), 128)
            raw = src[rows, :]
            turned = (raw * W[k, pl.ds(block, 1), :]).T
            high = turned.astype(BF16)
            LTh[at, rows] = high
            LTl[at, rows] = (turned - high.astype(F32)).astype(BF16)
            return squares + jnp.sum(raw * raw, axis=0, keepdims=True)

        before = RSQ[parity * 4 + r] if first else jnp.zeros((1, 128), F32)
        RSQ[parity * 4 + r] = lax.fori_loop(first, last, step, before)

    for r in range(4):
        wait_part(r, 0, oc, 0, None)
        for cs in (0, 1):
            wait_part(r, 1, cs, 0, None)
            wait_part(r, 3, cs, 0, None)
        send(R.at[0, r, 0:768], LO.at[r, 0:768], lo_s, lo_r.at[r, 0], dev(core=oc))
    arrived(W.at[slot(0, oc)], m_r.at[0, oc])
    for dx in (1, 2, 3):
        for cs in (0, 1):
            arrived(W.at[slot(dx, cs)], m_r.at[dx, cs])
    for r in range(4):
        left(R.at[0, r], r, c, 0, 6)
        arrived(LO.at[r, 0:768], lo_r.at[r, 0])
        left(LO.at[r], r, oc, 0, 6)
    for r in range(4):
        wait_relayed(r, 0)
        send(R.at[0, r, 768:1024], LO.at[r, 768:1024], lo_s, lo_r.at[r, 1], dev(core=oc))
        left(R.at[0, r], r, c, 6, 8)
    for r in range(4):
        arrived(LO.at[r, 768:1024], lo_r.at[r, 1])
        left(LO.at[r], r, oc, 6, 8)

    def product(*units):
        width = 128 * len(units)
        squares = []
        for j, (r, kq) in enumerate(units):
            src = R.at[kq, r]
            block = 2 * ((x + kq) % 4) + c
            at = slice(j * 128, j * 128 + 128)

            def split(i, total):
                rows = pl.ds(pl.multiple_of(i * 128, 128), 128)
                raw = src[rows, :]
                part = raw * W[i, pl.ds(block, 1), :]
                high = part.astype(BF16)
                RH[rows, at] = high
                RL[rows, at] = (part - high.astype(F32)).astype(BF16)
                return total + jnp.sum(raw * raw, axis=0, keepdims=True)

            squares.append(lax.fori_loop(0, 8, split, jnp.zeros((1, 128), F32)))

        def rows_of(m, carry):
            at = pl.ds(pl.multiple_of(m * 512, 512), 512)
            lh = LTh[at, :]
            rh = RH[:, 0:width]
            acc = jnp.dot(lh, rh, preferred_element_type=F32)
            acc += jnp.dot(LTl[at, :], rh, preferred_element_type=F32)
            acc += jnp.dot(lh, RL[:, 0:width], preferred_element_type=F32)
            for i in range(4):
                zd = 4 * m + i
                for j, (r, kq) in enumerate(units):
                    D[r, kq, zd, 0:128, :] = acc[i * 128 : i * 128 + 128, j * 128 : j * 128 + 128]
                    extra = jnp.where(lane_row == 0, squares[j], 0.0)
                    D[r, kq, zd, 128:ROWS, :] = jnp.where(lane_row == 1, RSQ[zd], extra)
            return carry

        lax.fori_loop(0, 2, rows_of, 0)

    def z_chain(chunk, buf, rs, ss, turn):
        def go(zd, j, way):
            send(chunk((z + zd * turn + 8) % 8), buf.at[j], ss, rs.at[j], dev(dz=way * turn))

        def take(j, zd):
            arrived(buf.at[j], rs.at[j])
            ref = chunk((z + zd * turn + 8) % 8)
            ref[...] += buf[j]

        def start():
            go(4, 0, 1)
            go(-3, 4, -1)

        def step1():
            take(0, 3)
            go(3, 1, 1)
            take(4, -2)
            go(-2, 5, -1)

        def step2():
            take(1, 2)
            go(2, 2, 1)
            take(5, -1)
            go(-1, 6, -1)

        def step3():
            take(2, 1)
            go(1, 3, 1)
            take(6, 0)

        def finish():
            take(3, 0)

        return start, step1, step2, step3, finish

    def y_chain(kq, ref, buf, rs, ss, turn):
        near, far = (1, 2) if turn == 1 else (2, 1)

        def go(j, way):
            send(ref, buf.at[j], ss.at[j], rs.at[j], dev(dy=(way * turn) % 4))

        def take(j):
            arrived(buf.at[j], rs.at[j])
            ref[...] += buf[j]

        def begin():
            @pl.when(kqs[0] == kq)
            def _():
                go(0, 1)

            @pl.when(kqs[far] == kq)
            def _():
                go(2, -1)

        def forward():
            @pl.when(kqs[near] == kq)
            def _():
                take(0)
                go(1, 1)

        def finish():
            @pl.when(own == kq)
            def _():
                take(2)
                take(1)

        return begin, forward, finish

    def y_sent(buf, ss, turn):
        for k, j in ((0, 0), (1, 1 if turn == 1 else 2), (2, 2 if turn == 1 else 1)):

            @pl.when(kqs[k] != 3)
            def _():
                all_sent(buf.at[j], ss.at[j])

    def zz(r, kq):
        i = r // 3
        return z_chain(lambda zd: D.at[r, kq, zd], ZRz.at[i, kq], zz_r.at[i, kq], zz_s.at[i, kq],
                       1 - 2 * ((kq + i) % 2))

    def zy(r, kq):
        i = r - 1
        return z_chain(lambda zd: D.at[r, kq, zd], ZRy.at[i], zy_r.at[i], zy_s.at[i], 1 - 2 * (r % 2 == 0))

    def yy(r, kq, t):
        i = r - 1
        return y_chain(kq, D.at[r, kq, t * 4 : t * 4 + 4], YR.at[i, t], yr_r.at[i, t], yr_s.at[i, t],
                       1 - 2 * t)

    def yz(r, kq):
        i = r // 3
        return y_chain(kq, D.at[r, kq, z], YRz.at[i], yz_r.at[i], yz_s.at[i], 1 - 2 * i)

    def cosines():
        row_rate = rate_ref[2 * x + z // 4]
        col_rate = rate_ref[2 * y + c]
        row_scale = row_rate * jnp.sqrt(D[0, own, z, 129:130, :] + EPS)
        row_scale = jnp.broadcast_to(row_scale, (128, 128)).T
        for r in range(4):
            col_scale = col_rate * jnp.sqrt(D[r, own, z, 128:129, :] + EPS)
            CF[:, r * 128 : r * 128 + 128] = D[r, own, z, 0:128, :] / (row_scale * col_scale)

    for name, *key in SCHEDULE:
        if name == "mul":
            for u in key:
                if u[1]:
                    wait_rest(*u)
            product(*key)
        elif name == "pass":
            pass_on(*key)
        elif name == "z":
            zz(*key[:2])[key[2]]()
        elif name == "yz":
            yz(*key[:2])[key[2]]()
        elif name == "y":
            yy(*key[:3])[key[3]]()
        elif name == "zy":

            @pl.when(own == key[1])
            def _():
                zy(*key[:2])[key[2]]()

        else:

            @pl.when(own == 1)
            def _():
                cosines()
                for g in range(4):
                    send(CF.at[:, g * 128 : g * 128 + 128], TB.at[zl], tb_s.at[g], tb_r.at[zl], takers[g])

    @pl.when((own == 0) | (own == 2))
    def _():
        cosines()

    @pl.when(own == 3)
    def _():
        for g in range(4):
            arrived(TB.at[g], tb_r.at[g])
            CF[:, g * 128 : g * 128 + 128] = TB[g].T

    half = pl.ds(pl.multiple_of(oc * 64, 64), 64)
    send(CF.at[half, :], out_ref.at[c], f_s, f_r, dev(core=oc))
    out_ref[c] = CF[pl.ds(pl.multiple_of(c * 64, 64), 64), :]
    arrived(out_ref.at[oc], f_r)
    all_sent(CF.at[half, :], f_s)
    for i in range(2):
        all_sent(a_ref.at[:, 0:3584], own_s.at[i])
        all_sent(a_ref.at[:, 0:1536], rel_s.at[i])
        y_sent(YRz.at[i], yz_s.at[i], 1 - 2 * i)
        for t in range(2):
            y_sent(YR.at[i, t], yr_s.at[i, t], 1 - 2 * t)
        for kq in range(3):
            all_sent(ZRz.at[i, kq], zz_s.at[i, kq])

        @pl.when(own != 3)
        def _():
            all_sent(ZRy.at[i], zy_s.at[i])

    @pl.when(own == 1)
    def _():
        for g in range(4):
            all_sent(TB.at[g], tb_s.at[g])

    all_sent(a_ref.at[:, 0:1536], sib_s)
    all_sent(LO, lo_s)
    for i in [0] + list(range(2, 8)):
        all_sent(w_ref, m_s.at[i])


def per_device(samples, keep_mask, keep_rate):
    dma = pltpu.SemaphoreType.DMA
    vmem = pltpu.VMEM
    return pl.pallas_call(
        kernel,
        out_shape=jax.ShapeDtypeStruct((2, 64, 512), F32),
        in_specs=[
            pl.BlockSpec(memory_space=pl.ANY),
            pl.BlockSpec(memory_space=pltpu.SMEM),
            pl.BlockSpec(memory_space=pltpu.SMEM),
        ],
        out_specs=pl.BlockSpec(memory_space=pltpu.VMEM),
        scratch_shapes=[
            vmem((128, 4096), F32),
            vmem((4, 4, 1024, 128), F32),
            vmem((4, 1024, 128), F32),
            vmem((8, 8, 128), F32),
            vmem((1024, 1024), BF16),
            vmem((1024, 1024), BF16),
            vmem((1024, 256), BF16),
            vmem((1024, 256), BF16),
            vmem((4, 4, 8, ROWS, 128), F32),
            vmem((8, 1, 128), F32),
            vmem((2, 2, 3, 4, ROWS, 128), F32),
            vmem((2, 3, ROWS, 128), F32),
            vmem((2, 7, ROWS, 128), F32),
            vmem((2, 3, 7, ROWS, 128), F32),
            vmem((128, 512), F32),
            vmem((4, 128, 128), F32),
            dma((4, 4, 2, 4, 2)),
            dma((4, 2, 2, 4)),
            dma((4, 2)),
            dma((4, 2)),
            dma((2, 2, 3)),
            dma((2, 3)),
            dma((2, 7)),
            dma((2, 3, 7)),
            dma((4,)),
            dma,
            dma((2,)),
            dma((2,)),
            dma,
            dma,
            dma((8,)),
            dma((2, 2, 3)),
            dma((2, 3)),
            dma((2,)),
            dma((2, 3)),
            dma((4,)),
            dma,
            dma,
        ],
        compiler_params=pltpu.CompilerParams(
            collective_id=0, has_side_effects=True, vmem_limit_bytes=60 << 20
        ),
        name="sampled_gram",
    )(samples, keep_mask, keep_rate)


def solution(mesh):
    finer = Mesh(mesh.devices.reshape(4, 2, 4, 4, 2), AXES)
    rows = P(AXES, None)
    return jax.shard_map(
        per_device,
        mesh=finer,
        in_specs=(rows, rows, P()),
        out_specs=P(("x", "zh", "y"), ("zl", "c"), None),
        check_vma=False,
    )
```
